256 devices in a mesh: seq: 64 (over y, z, core), ch: 4 (over x).
Axes of the slice: x: 4, y: 4, z: 8, core: 2. Of those that a mesh axis runs over, the one named last changes fastest.
Arguments:
- inputs: bfloat16 [512, 512, 1024], P('seq', None, 'ch'), may hold values from -6 to 6
- cotangent: bfloat16 [512, 512, 1024], P(None, 'seq', 'ch'), may hold values from -6 to 6
- right_weight: bfloat16 [512, 512], replicated, may hold values from -0.25 to 0.25
- left_weight: bfloat16 [512, 512], replicated, may hold values from -0.25 to 0.25
- first_gate: bfloat16 [512, 1024], P(None, 'ch'), may hold values from -4 to 4
- second_gate: bfloat16 [512, 1024], P(None, 'ch'), may hold values from -4 to 4
Outputs:
- output: bfloat16 [512, 512, 1024], P(None, 'seq', 'ch')
- grad_inputs: bfloat16 [512, 512, 1024], P('seq', None, 'ch')
- grad_right: float32 [512, 512], P(('seq', 'ch'))
- grad_left: float32 [512, 512], P(('seq', 'ch'))
- grad_first_gate: float32 [512, 1024], P('seq', 'ch')
- grad_second_gate: float32 [512, 1024], P('seq', 'ch')
The draws below stay inside these ranges and needn't reach their ends.
All inputs are finite; a program needn't handle non-finite values.
Results may differ from the reference program's by a relative error of at most 0.015.
Values may be sent and summed in bfloat16 or wider, within the bound.
A program may use at most 64 MiB of HBM per device.

```python
import math
import jax
import jax.numpy as jnp
from jax import lax

GRID_ROWS = 512
GRID_COLS = 512
CHANNELS = 1024


def levels(stream_key, extent, cuts, smallest, high):
    level = 1.0
    for dim, parts in cuts:
        heights = jax.random.uniform(jax.random.fold_in(jax.random.fold_in(stream_key, 6), dim), (parts,), jnp.float32, smallest / len(cuts), high / len(cuts))
        level = level * jnp.repeat(jnp.exp(heights), extent[dim] // parts).reshape((-1,) + (1,) * (len(extent) - 1 - dim))
    return level


def bell_draw(stream_key, dims, deviation, limit, pieces=(), held_as=jnp.bfloat16):
    drawn = jax.random.normal(stream_key, dims, jnp.float32) * deviation
    if len(pieces) > 0:
        drawn = levels(stream_key, dims, pieces, -0.22, 0.18) * drawn
    return jnp.clip(drawn, min=-limit, max=limit).astype(held_as)


def setup_inputs(seed: int = 0) -> dict:
    key_of = jax.random.split(jax.random.key(seed), 7)
    return {
        "inputs": bell_draw(key_of[0], (GRID_ROWS, GRID_COLS, CHANNELS), 1.0, 6.0, ((0, 64), (2, 4))),
        "cotangent": bell_draw(key_of[1], (GRID_ROWS, GRID_COLS, CHANNELS), 1.0, 6.0, ((1, 64), (2, 4))),
        "right_weight": bell_draw(key_of[2], (GRID_COLS, GRID_COLS), GRID_COLS ** -0.5, 0.25),
        "left_weight": bell_draw(key_of[3], (GRID_ROWS, GRID_ROWS), GRID_ROWS ** -0.5, 0.25),
        "first_gate": bell_draw(key_of[4], (GRID_COLS, CHANNELS), 1.0, 4.0, ((1, 4),)),
        "second_gate": bell_draw(key_of[5], (GRID_ROWS, CHANNELS), 1.0, 4.0, ((1, 4),)),
    }


def block_pass(right32, left32, inputs, cotangent, first_gate, second_gate):
    section_one = jnp.einsum("kj,ijc->ikc", right32, inputs.astype(jnp.float32)).astype(jnp.bfloat16)
    gate_one = first_gate.astype(jnp.float32)[None, :, :]
    panels = (section_one.astype(jnp.float32) * gate_one).astype(jnp.bfloat16)
    mixed = jnp.einsum("mi,ikc->mkc", left32, panels.astype(jnp.float32))
    logistic = jax.nn.sigmoid(mixed)
    activated = mixed * logistic
    gate_two = second_gate.astype(jnp.float32)[:, None, :]
    output = (activated * gate_two).astype(jnp.bfloat16)
    grad_out = cotangent.astype(jnp.float32)
    grad_second = jnp.sum(grad_out * activated, axis=1)
    grad_mixed = (grad_out * gate_two * logistic * (1.0 + mixed * (1.0 - logistic))).astype(jnp.bfloat16)
    grad_left = jnp.einsum("mkc,ikc->mi", grad_mixed.astype(jnp.float32), panels.astype(jnp.float32))
    grad_panels = jnp.einsum("mi,mkc->ikc", left32, grad_mixed.astype(jnp.float32)).astype(jnp.bfloat16)
    grad_first = jnp.sum(grad_panels.astype(jnp.float32) * section_one.astype(jnp.float32), axis=0)
    grad_section = (grad_panels.astype(jnp.float32) * gate_one).astype(jnp.bfloat16)
    grad_inputs = jnp.einsum("kj,ikc->ijc", right32, grad_section.astype(jnp.float32)).astype(jnp.bfloat16)
    grad_right = jnp.einsum("ikc,ijc->kj", grad_section.astype(jnp.float32), inputs.astype(jnp.float32))
    return output, grad_inputs, grad_right, grad_left, grad_first, grad_second


def reference(inputs, cotangent, right_weight, left_weight, first_gate, second_gate):
    width = math.gcd(CHANNELS, 128)
    groups = CHANNELS // width
    right32 = right_weight.astype(jnp.float32)
    left32 = left_weight.astype(jnp.float32)

    def split(array):
        return jnp.moveaxis(array.reshape(array.shape[:-1] + (groups, width)), -2, 0)

    def joined(array):
        moved = jnp.moveaxis(array, 0, -2)
        return moved.reshape(moved.shape[:-2] + (CHANNELS,))

    def step(carry, blocks):
        output, grad_inputs, grad_right, grad_left, grad_first, grad_second = block_pass(right32, left32, blocks[0], blocks[1], blocks[2], blocks[3])
        return (carry[0] + grad_right, carry[1] + grad_left), (output, grad_inputs, grad_first, grad_second)

    start = (jnp.zeros((GRID_COLS, GRID_COLS), jnp.float32), jnp.zeros((GRID_ROWS, GRID_ROWS), jnp.float32))
    totals, stacked = lax.scan(step, start, (split(inputs), split(cotangent), split(first_gate), split(second_gate)))
    return (joined(stacked[0]), joined(stacked[1]), totals[0], totals[1], joined(stacked[2]), joined(stacked[3]))
```

```python
import jax
import jax.numpy as jnp
from jax import lax
from jax.sharding import PartitionSpec as P


def per_device(inputs, cotangent, right_weight, left_weight, first_gate, second_gate):
    section_one = jnp.einsum(
        "kj,ijd->ikd", right_weight, inputs, preferred_element_type=jnp.float32
    ).astype(jnp.bfloat16)
    gate_one = first_gate.astype(jnp.float32)[None, :, :]
    panels = (section_one.astype(jnp.float32) * gate_one).astype(jnp.bfloat16)
    received = lax.all_to_all(panels, "seq", split_axis=1, concat_axis=0, tiled=True)
    mixed = jnp.einsum("mi,ikd->mkd", left_weight, received, preferred_element_type=jnp.float32)
    logistic = jax.nn.sigmoid(mixed)
    activated = mixed * logistic
    gate_two = second_gate.astype(jnp.float32)[:, None, :]
    output = (activated * gate_two).astype(jnp.bfloat16)
    grad_out = cotangent.astype(jnp.float32)
    second_part = jnp.sum(grad_out * activated, axis=1)
    grad_mixed = (grad_out * gate_two * logistic * (1.0 + mixed * (1.0 - logistic))).astype(
        jnp.bfloat16
    )
    left_part = jnp.einsum("mkd,ikd->mi", grad_mixed, received, preferred_element_type=jnp.float32)
    early = lax.psum_scatter(
        jnp.concatenate([left_part, second_part], axis=1), "seq", scatter_dimension=0, tiled=True
    )
    order = left_part.shape[1]
    grad_left = lax.psum_scatter(early[:, :order], "ch", scatter_dimension=0, tiled=True)
    grad_second = early[:, order:]
    grad_panels = jnp.einsum(
        "mi,mkd->ikd", left_weight, grad_mixed, preferred_element_type=jnp.float32
    ).astype(jnp.bfloat16)
    returned = lax.all_to_all(grad_panels, "seq", split_axis=0, concat_axis=1, tiled=True)
    returned32 = returned.astype(jnp.float32)
    first_part = jnp.sum(returned32 * section_one.astype(jnp.float32), axis=0)
    grad_section = (returned32 * gate_one).astype(jnp.bfloat16)
    grad_inputs = jnp.einsum(
        "kj,ikd->ijd", right_weight, grad_section, preferred_element_type=jnp.float32
    ).astype(jnp.bfloat16)
    right_part = jnp.einsum("ikd,ijd->kj", grad_section, inputs, preferred_element_type=jnp.float32)
    late = lax.psum_scatter(
        jnp.concatenate([right_part, first_part], axis=1), "seq", scatter_dimension=0, tiled=True
    )
    order = right_part.shape[1]
    grad_right = lax.psum_scatter(late[:, :order], "ch", scatter_dimension=0, tiled=True)
    grad_first = late[:, order:]
    return (output, grad_inputs, grad_right, grad_left, grad_first, grad_second)


def solution(mesh):
    placed = (P("seq", None, "ch"), P(None, "seq", "ch"), P(), P(), P(None, "ch"), P(None, "ch"))
    return jax.shard_map(
        per_device,
        mesh=mesh,
        in_specs=placed,
        out_specs=(
            P(None, "seq", "ch"),
            P("seq", None, "ch"),
            P(("seq", "ch"), None),
            P(("seq", "ch"), None),
            P("seq", "ch"),
            P("seq", "ch"),
        ),
        check_vma=False,
    )
```

```python
import functools

import jax
import jax.numpy as jnp
from jax import lax
from jax.experimental import pallas as pl
from jax.experimental.pallas import tpu as pltpu
from jax.sharding import PartitionSpec as P

MESH = pl.DeviceIdType.MESH
F32 = jnp.float32
BF16 = jnp.bfloat16
LANES = 128
ROWS = 64


def dot(a, b, contract):
    return lax.dot_general(a, b, ((contract[:1], contract[1:]), ((), ())), preferred_element_type=F32)


def fused(
    seqs, chs, grid,
    x_hbm, ct_hbm, right_hbm, left_hbm, gate1_hbm, gate2_hbm,
    out_hbm, gi_hbm, gr_out, gl_out, gf_out, gs_out,
    xv, ctv, right, left, gate1, gate2, ov, giv,
    right_t, left_t, s1, flat, flat_out, prod, pair, grad_pair, gl, gr, gfirst, gsecond,
    fsend, frecv, bsend, brecv,
    csend, crecv, cgsend, cgrecv, half, xsend, xrecv, quarter, zsend, zrecv, zgsend, zgrecv,
    in_sem, out_sem, fs_sem, fr_sem, bs_sem, br_sem, r_sem,
):
    s, ch = lax.axis_index("seq"), lax.axis_index("ch")
    core = s % 2
    own = s // 2
    pairs = seqs // 2
    blocks = grid // ROWS

    barrier = pltpu.get_barrier_semaphore()

    def greet(t, _):
        pl.semaphore_signal(barrier, inc=1, device_id=((s + t) % seqs, ch), device_id_type=MESH)
        return 0

    def greet_ch(t, _):
        pl.semaphore_signal(barrier, inc=1, device_id=(s, (ch + t) % chs), device_id_type=MESH)
        return 0

    loads = [
        pltpu.make_async_copy(src, dst, in_sem.at[n])
        for n, (src, dst) in enumerate(
            ((x_hbm, xv), (right_hbm, right), (gate1_hbm, gate1), (ct_hbm, ctv), (left_hbm, left), (gate2_hbm, gate2))
        )
    ]
    for load in loads:
        load.start()
    lax.fori_loop(1, seqs, greet, 0)
    lax.fori_loop(1, chs, greet_ch, 0)
    for load in loads[:3]:
        load.wait()

    def half_of(h):
        return slice(h * LANES, (h + 1) * LANES)

    def x_pair(h, ip):
        return jnp.concatenate([xv[2 * ip, :, half_of(h)], xv[2 * ip + 1, :, half_of(h)]], axis=1)

    def exchange(h, src, dst, send_sem, recv_sem):
        pltpu.make_async_copy(src.at[h, s], dst.at[h, s], recv_sem.at[h]).start()

        def send(t, _):
            d = (s + t) % seqs
            pltpu.make_async_remote_copy(
                src_ref=src.at[h, d], dst_ref=dst.at[h, s], send_sem=send_sem.at[h], recv_sem=recv_sem.at[h],
                device_id=(d, ch), device_id_type=MESH,
            ).start()
            return 0

        lax.fori_loop(1, seqs, send, 0)

    def arrived(dst, sem):
        pltpu.make_async_copy(dst, dst, sem).wait()

    def first_stage(h):
        def per_pair(ip, _):
            prod[...] = dot(right[...], x_pair(h, ip), (1, 0))

            def rows(b, _):
                r = pl.ds(pl.multiple_of(b * ROWS, ROWS), ROWS)
                gate = gate1[r, half_of(h)].astype(F32)
                for e in range(2):
                    section = prod[r, half_of(e)].astype(BF16)
                    s1[2 * ip + e, h, r, :] = section
                    flat[pl.ds(b * (ROWS * 8) + 2 * ip + e, ROWS, stride=8), :] = section.astype(F32) * gate
                return 0

            lax.fori_loop(0, blocks, rows, 0)
            return 0

        lax.fori_loop(0, 4, per_pair, 0)

        def pack(d, _):
            rows = flat[pl.ds(pl.multiple_of(d * 64, 64), 64), :]
            fsend[h, d] = rows.reshape(8, 8, LANES).astype(BF16)
            return 0

        lax.fori_loop(0, seqs, pack, 0, unroll=4)

    def middle(h):
        def unpack(b, _):
            m = pl.ds(pl.multiple_of(b * 8, 8), 8)
            flat[pl.ds(pl.multiple_of(b * 64, 64), 64), :] = ctv[m, :, half_of(h)].astype(F32).reshape(64, LANES)
            return 0

        lax.fori_loop(0, grid // 8, unpack, 0, unroll=4)
        gsecond[:, half_of(h)] = jnp.zeros((grid, LANES), F32)
        arrived(frecv.at[h], fr_sem.at[h])

        def per_pair(kp, _):
            pair[...] = jnp.concatenate(
                [frecv[h, :, 2 * kp + e].astype(F32).reshape(grid, LANES).astype(BF16) for e in range(2)], axis=1
            )
            prod[...] = dot(left[...], pair[...], (1, 0))

            def rows(b, _):
                r = pl.ds(pl.multiple_of(b * ROWS, ROWS), ROWS)
                gate = gate2[r, half_of(h)].astype(F32)
                total = gsecond[r, half_of(h)]
                for e in range(2):
                    at = pl.ds(b * (ROWS * 8) + 2 * kp + e, ROWS, stride=8)
                    mixed = prod[r, half_of(e)]
                    grad_out = flat[at, :]
                    logistic = 1.0 / (1.0 + jnp.exp(-mixed))
                    activated = mixed * logistic
                    flat_out[at, :] = activated * gate
                    total = total + grad_out * activated
                    grad_mixed = grad_out * gate * logistic * (1.0 + mixed * (1.0 - logistic))
                    grad_pair[r, half_of(e)] = grad_mixed.astype(BF16)
                gsecond[r, half_of(h)] = total
                return 0

            lax.fori_loop(0, blocks, rows, 0)
            gl[...] += dot(grad_pair[...], pair[...], (1, 1))
            prod[...] = dot(left_t[...], grad_pair[...], (1, 0))
            for e in range(2):
                bsend[h, :, 2 * kp + e] = prod[:, half_of(e)].reshape(seqs, 8, LANES).astype(BF16)
            return 0

        lax.fori_loop(0, 4, per_pair, 0)

    def write_out(h):
        def pack(b, _):
            m = pl.ds(pl.multiple_of(b * 8, 8), 8)
            rows = flat_out[pl.ds(pl.multiple_of(b * 64, 64), 64), :]
            ov[m, :, half_of(h)] = rows.reshape(8, 8, LANES).astype(BF16)
            return 0

        lax.fori_loop(0, grid // 8, pack, 0, unroll=4)

    def last_stage(h):
        gfirst[:, half_of(h)] = jnp.zeros((grid, LANES), F32)
        arrived(brecv.at[h], br_sem.at[h])

        def unpack(b, _):
            rows = brecv[h, b].astype(F32).reshape(64, LANES)
            flat[pl.ds(pl.multiple_of(b * 64, 64), 64), :] = rows
            return 0

        lax.fori_loop(0, seqs, unpack, 0, unroll=4)

        def per_pair(ip, _):
            def rows(b, _):
                r = pl.ds(pl.multiple_of(b * ROWS, ROWS), ROWS)
                gate = gate1[r, half_of(h)].astype(F32)
                total = gfirst[r, half_of(h)]
                for e in range(2):
                    grad = flat[pl.ds(b * (ROWS * 8) + 2 * ip + e, ROWS, stride=8), :]
                    total = total + grad * s1[2 * ip + e, h, r, :].astype(F32)
                    grad_pair[r, half_of(e)] = (grad * gate).astype(BF16)
                gfirst[r, half_of(h)] = total
                return 0

            lax.fori_loop(0, blocks, rows, 0)
            gr[...] += dot(grad_pair[...], x_pair(h, ip), (1, 1))
            prod[...] = dot(right_t[...], grad_pair[...], (1, 0))
            for e in range(2):
                giv[2 * ip + e, :, half_of(h)] = prod[:, half_of(e)].astype(BF16)
            return 0

        lax.fori_loop(0, 4, per_pair, 0)

    def reduce(n, matrix, gates, matrix_out, gates_out):
        sems = r_sem.at[n]

        def give(p, _):
            r = pl.ds(pl.multiple_of(p * 16 + (1 - core) * 8, 8), 8)
            csend[n, p] = matrix[r, :].astype(BF16)
            cgsend[n, p] = gates[r, :].astype(BF16)
            return 0

        lax.fori_loop(0, pairs, give, 0, unroll=2)
        copies = [
            pltpu.make_async_remote_copy(
                src_ref=src.at[n], dst_ref=dst.at[n], send_sem=sems.at[2 * q], recv_sem=sems.at[2 * q + 1],
                device_id=(s + 1 - 2 * core, ch), device_id_type=MESH,
            )
            for q, (src, dst) in enumerate(((csend, crecv), (cgsend, cgrecv)))
        ]
        for copy in copies:
            copy.start()
        for copy in copies:
            copy.wait()

        def take(p, _):
            r = pl.ds(pl.multiple_of(p * 16 + core * 8, 8), 8)
            total = matrix[r, :] + crecv[n, p].astype(F32)
            for c in range(4):
                half[c, pl.ds(pl.multiple_of(p * 8, 8), 8), :] = total[:, c * LANES : (c + 1) * LANES]
            zgsend[n, p] = (gates[r, :] + cgrecv[n, p].astype(F32)).astype(BF16)
            return 0

        lax.fori_loop(0, pairs, take, 0, unroll=2)
        for a in range(chs):
            for b in range(2):
                for c in range(4):
                    lanes = slice(c * LANES, (c + 1) * LANES)
                    xsend[n, a, b, :, lanes] = half[c, pl.ds(2 * a + b, pairs, stride=8), :].astype(BF16)
        pltpu.make_async_copy(xsend.at[n, ch], xrecv.at[n, ch], sems.at[5]).start()

        def send_ch(t, _):
            d = (ch + t) % chs
            pltpu.make_async_remote_copy(
                src_ref=xsend.at[n, d], dst_ref=xrecv.at[n, ch], send_sem=sems.at[4], recv_sem=sems.at[5],
                device_id=(s, d), device_id_type=MESH,
            ).start()
            return 0

        lax.fori_loop(1, chs, send_ch, 0)
        pltpu.make_async_copy(zgsend.at[n, own], zgrecv.at[n, own], sems.at[9]).start()

        def send_gates(t, _):
            d = (own + t) % pairs
            pltpu.make_async_remote_copy(
                src_ref=zgsend.at[n, d], dst_ref=zgrecv.at[n, own], send_sem=sems.at[8], recv_sem=sems.at[9],
                device_id=(2 * d + core, ch), device_id_type=MESH,
            ).start()
            return 0

        lax.fori_loop(1, pairs, send_gates, 0)
        arrived(xrecv.at[n], sems.at[5])
        total = xrecv[n, 0].astype(F32)
        for a in range(1, chs):
            total = total + xrecv[n, a].astype(F32)
        for c in range(4):
            quarter[c] = total.reshape(2 * pairs, grid)[:, c * LANES : (c + 1) * LANES]
        for p in range(pairs):
            for c in range(4):
                lanes = slice(c * LANES, (c + 1) * LANES)
                zsend[n, p, :, lanes] = quarter[c, pl.ds(p, 2, stride=pairs), :].astype(BF16)
        pltpu.make_async_copy(zsend.at[n, own], zrecv.at[n, own], sems.at[7]).start()

        def send_rows(t, _):
            d = (own + t) % pairs
            pltpu.make_async_remote_copy(
                src_ref=zsend.at[n, d], dst_ref=zrecv.at[n, own], send_sem=sems.at[6], recv_sem=sems.at[7],
                device_id=(2 * d + core, ch), device_id_type=MESH,
            ).start()
            return 0

        lax.fori_loop(1, pairs, send_rows, 0)
        arrived(zgrecv.at[n], sems.at[9])
        gates_out[...] = jnp.sum(zgrecv[n].astype(F32), axis=0)
        arrived(zrecv.at[n], sems.at[7])
        matrix_out[...] = jnp.sum(zrecv[n].astype(F32), axis=0)
        arrived(xsend.at[n, pl.ds(0, chs - 1)], sems.at[4])
        arrived(zsend.at[n, pl.ds(0, pairs - 1)], sems.at[6])
        arrived(zgsend.at[n, pl.ds(0, pairs - 1)], sems.at[8])

    first_stage(0)
    pl.semaphore_wait(barrier, seqs + chs - 2)
    exchange(0, fsend, frecv, fs_sem, fr_sem)
    first_stage(1)
    exchange(1, fsend, frecv, fs_sem, fr_sem)
    for load in loads[3:]:
        load.wait()
    right_t[...] = right[...].T
    left_t[...] = left[...].T
    gl[...] = jnp.zeros(gl.shape, F32)
    gr[...] = jnp.zeros(gr.shape, F32)
    stores = []
    for h in range(2):
        middle(h)
        exchange(h, bsend, brecv, bs_sem, br_sem)
        write_out(h)
    store = pltpu.make_async_copy(ov, out_hbm, out_sem.at[0])
    store.start()
    stores.append(store)
    reduce(0, gl, gsecond, gl_out, gs_out)
    for h in range(2):
        last_stage(h)
    store = pltpu.make_async_copy(giv, gi_hbm, out_sem.at[1])
    store.start()
    stores.append(store)
    reduce(1, gr, gfirst, gr_out, gf_out)
    for store in stores:
        store.wait()
    for h in range(2):
        arrived(fsend.at[h, pl.ds(0, seqs - 1)], fs_sem.at[h])
        arrived(bsend.at[h, pl.ds(0, seqs - 1)], bs_sem.at[h])


def per_device(seqs, chs, inputs, cotangent, right_weight, left_weight, first_gate, second_gate):
    rows, grid, width = inputs.shape
    hbm = pl.BlockSpec(memory_space=pl.ANY)
    vmem = pl.BlockSpec(memory_space=pltpu.VMEM)
    pairs = seqs // 2
    block = (2, seqs, 8, 8, LANES)

    def v(shape, dtype=BF16):
        return pltpu.VMEM(shape, dtype)

    dma = pltpu.SemaphoreType.DMA
    out, gi, gr, gl, gf, gs = pl.pallas_call(
        functools.partial(fused, seqs, chs, grid),
        out_shape=(
            jax.ShapeDtypeStruct(cotangent.shape, BF16),
            jax.ShapeDtypeStruct(inputs.shape, BF16),
            jax.ShapeDtypeStruct((2, grid), F32),
            jax.ShapeDtypeStruct((2, grid), F32),
            jax.ShapeDtypeStruct((8, width), F32),
            jax.ShapeDtypeStruct((8, width), F32),
        ),
        in_specs=[hbm] * 6,
        out_specs=(hbm, hbm, vmem, vmem, vmem, vmem),
        scratch_shapes=[
            v(inputs.shape), v(cotangent.shape), v((grid, grid)), v((grid, grid)), v((grid, width)), v((grid, width)),
            v(cotangent.shape), v(inputs.shape),
            v((grid, grid)), v((grid, grid)), v((8, 2, grid, LANES)), v((grid * 8, LANES), F32), v((grid * 8, LANES), F32),
            v((grid, 2 * LANES), F32), v((grid, 2 * LANES)), v((grid, 2 * LANES)),
            v((grid, grid), F32), v((grid, grid), F32), v((grid, width), F32), v((grid, width), F32),
            v(block), v(block), v(block), v(block),
            v((2, pairs, 8, grid)), v((2, pairs, 8, grid)), v((2, pairs, 8, width)), v((2, pairs, 8, width)),
            v((4, pairs * 8, LANES), F32), v((2, chs, 2, pairs, grid)), v((2, chs, 2, pairs, grid)),
            v((4, 2 * pairs, LANES), F32), v((2, pairs, 2, grid)), v((2, pairs, 2, grid)),
            v((2, pairs, 8, width)), v((2, pairs, 8, width)),
            dma((6,)), dma((2,)), dma((2,)), dma((2,)), dma((2,)), dma((2,)), dma((2, 10)),
        ],
        compiler_params=pltpu.CompilerParams(
            collective_id=0, has_side_effects=True, vmem_limit_bytes=60 * 1024 * 1024
        ),
    )(inputs, cotangent, right_weight, left_weight, first_gate, second_gate)
    return out, gi, gr, gl, gf, gs


def solution(mesh):
    placed = (P("seq", None, "ch"), P(None, "seq", "ch"), P(), P(), P(None, "ch"), P(None, "ch"))
    return jax.shard_map(
        functools.partial(per_device, mesh.shape["seq"], mesh.shape["ch"]),
        mesh=mesh,
        in_specs=placed,
        out_specs=(
            P(None, "seq", "ch"),
            P("seq", None, "ch"),
            P(("seq", "ch"), None),
            P(("seq", "ch"), None),
            P("seq", "ch"),
            P("seq", "ch"),
        ),
        check_vma=False,
    )
```

```python
import functools

import jax
import jax.numpy as jnp
from jax import lax
from jax.experimental import pallas as pl
from jax.experimental.pallas import tpu as pltpu
from jax.sharding import PartitionSpec as P

MESH = pl.DeviceIdType.MESH
F32 = jnp.float32
BF16 = jnp.bfloat16
LANES = 128
ROWS = 64
CHIPS_Z = 8
LIMIT_MIB = 44


def dot(a, b, contract):
    return lax.dot_general(a, b, ((contract[:1], contract[1:]), ((), ())), preferred_element_type=F32)


def fused(
    seqs, zs, chs, grid,
    x_hbm, ct_hbm, right_hbm, left_hbm, gate1_hbm, gate2_hbm,
    ov, giv, gr_out, gl_out, gf_out, gs_out,
    xv, ctv, right, left, gate1, gate2,
    right_t, left_t, s1, flat, flat_out, prod, pair, grad_pair, section, gl, gr, gfirst, gsecond,
    fsend, frecv, bsend, brecv,
    csend, crecv, cgsend, cgrecv, half, xsend, xrecv, ysend, yrecv, ygsend, ygrecv, thin, zsend, zrecv, zgsend, zgrecv,
    in_sem, fs_sem, fr_sem, bs_sem, br_sem, r_sem,
):
    s, ch = lax.axis_index("seq"), lax.axis_index("ch")
    core = s % 2
    own_y, own_z = s // (2 * zs), (s // 2) % zs
    ys = seqs // (2 * zs)
    pairs = seqs // 2
    blocks = grid // ROWS

    barrier = pltpu.get_barrier_semaphore()

    def greet(t, _):
        pl.semaphore_signal(barrier, inc=1, device_id=((s + t) % seqs, ch), device_id_type=MESH)
        return 0

    def greet_ch(t, _):
        pl.semaphore_signal(barrier, inc=1, device_id=(s, (ch + t) % chs), device_id_type=MESH)
        return 0

    loads = [
        pltpu.make_async_copy(src, dst, in_sem.at[n])
        for n, (src, dst) in enumerate(
            ((x_hbm, xv), (right_hbm, right), (gate1_hbm, gate1), (ct_hbm, ctv), (left_hbm, left), (gate2_hbm, gate2))
        )
    ]
    for load in loads:
        load.start()
    lax.fori_loop(1, seqs, greet, 0)
    lax.fori_loop(1, chs, greet_ch, 0)
    for load in loads[:3]:
        load.wait()

    def half_of(h):
        return slice(h * LANES, (h + 1) * LANES)

    def x_pair(h, ip):
        return jnp.concatenate([xv[2 * ip, :, half_of(h)], xv[2 * ip + 1, :, half_of(h)]], axis=1)

    def turn(n, extent):
        odd = n % 2
        return (odd * ((n + 1) // 2) + (1 - odd) * (extent - n // 2)) % extent

    def far_first(t):
        z = (own_z + turn(t % zs, zs)) % zs
        y = (own_y + turn(t // zs % ys, ys)) % ys
        return (y * zs + z) * 2 + (core + t // (zs * ys)) % 2

    def exchange(h, src, dst, send_sem, recv_sem):
        pltpu.make_async_copy(src.at[h, s], dst.at[h, s], recv_sem.at[h]).start()

        def send(t, _):
            d = far_first(seqs - t)
            pltpu.make_async_remote_copy(
                src_ref=src.at[h, d], dst_ref=dst.at[h, s], send_sem=send_sem.at[h], recv_sem=recv_sem.at[h],
                device_id=(d, ch), device_id_type=MESH,
            ).start()
            return 0

        lax.fori_loop(1, seqs, send, 0)

    def arrived(dst, sem):
        pltpu.make_async_copy(dst, dst, sem).wait()

    def first_stage(h):
        def per_pair(ip, _):
            prod[...] = dot(right[...], x_pair(h, ip), (1, 0))

            def rows(b, _):
                r = pl.ds(pl.multiple_of(b * ROWS, ROWS), ROWS)
                gate = gate1[r, half_of(h)].astype(F32)
                for e in range(2):
                    rounded = prod[r, half_of(e)].astype(BF16)
                    s1[2 * ip + e, h, r, :] = rounded
                    flat[pl.ds(b * (ROWS * 8) + 2 * ip + e, ROWS, stride=8), :] = rounded.astype(F32) * gate
                return 0

            lax.fori_loop(0, blocks, rows, 0)
            return 0

        lax.fori_loop(0, 4, per_pair, 0)

        def pack(d, _):
            rows = flat[pl.ds(pl.multiple_of(d * 64, 64), 64), :]
            fsend[h, d] = rows.reshape(8, 8, LANES).astype(BF16)
            return 0

        lax.fori_loop(0, seqs, pack, 0, unroll=4)

    def middle(h):
        def unpack(b, _):
            m = pl.ds(pl.multiple_of(b * 8, 8), 8)
            flat[pl.ds(pl.multiple_of(b * 64, 64), 64), :] = ctv[m, :, half_of(h)].astype(F32).reshape(64, LANES)
            return 0

        lax.fori_loop(0, grid // 8, unpack, 0, unroll=4)
        gsecond[:, half_of(h)] = jnp.zeros((grid, LANES), F32)
        arrived(frecv.at[h], fr_sem.at[h])

        def per_pair(kp, _):
            pair[...] = jnp.concatenate(
                [frecv[h, :, 2 * kp + e].astype(F32).reshape(grid, LANES).astype(BF16) for e in range(2)], axis=1
            )
            prod[...] = dot(left[...], pair[...], (1, 0))

            def rows(b, _):
                r = pl.ds(pl.multiple_of(b * ROWS, ROWS), ROWS)
                gate = gate2[r, half_of(h)].astype(F32)
                total = gsecond[r, half_of(h)]
                for e in range(2):
                    at = pl.ds(b * (ROWS * 8) + 2 * kp + e, ROWS, stride=8)
                    mixed = prod[r, half_of(e)]
                    grad_out = flat[at, :]
                    logistic = 1.0 / (1.0 + jnp.exp(-mixed))
                    activated = mixed * logistic
                    flat_out[at, :] = activated * gate
                    total = total + grad_out * activated
                    grad_mixed = grad_out * gate * logistic * (1.0 + mixed * (1.0 - logistic))
                    grad_pair[r, half_of(e)] = grad_mixed.astype(BF16)
                gsecond[r, half_of(h)] = total
                return 0

            lax.fori_loop(0, blocks, rows, 0)
            gl[...] += dot(grad_pair[...], pair[...], (1, 1))
            prod[...] = dot(left_t[...], grad_pair[...], (1, 0))
            for e in range(2):
                bsend[h, :, 2 * kp + e] = prod[:, half_of(e)].reshape(seqs, 8, LANES).astype(BF16)
            return 0

        lax.fori_loop(0, 4, per_pair, 0)

    def write_out(h):
        def pack(b, _):
            m = pl.ds(pl.multiple_of(b * 8, 8), 8)
            rows = flat_out[pl.ds(pl.multiple_of(b * 64, 64), 64), :]
            ov[m, :, half_of(h)] = rows.reshape(8, 8, LANES).astype(BF16)
            return 0

        lax.fori_loop(0, grid // 8, pack, 0, unroll=4)

    def last_stage(h):
        gfirst[:, half_of(h)] = jnp.zeros((grid, LANES), F32)
        arrived(brecv.at[h], br_sem.at[h])

        def unpack(b, _):
            rows = brecv[h, b].astype(F32).reshape(64, LANES)
            flat[pl.ds(pl.multiple_of(b * 64, 64), 64), :] = rows
            return 0

        lax.fori_loop(0, seqs, unpack, 0, unroll=4)

        def per_pair(ip, _):
            def rows(b, _):
                r = pl.ds(pl.multiple_of(b * ROWS, ROWS), ROWS)
                gate = gate1[r, half_of(h)].astype(F32)
                total = gfirst[r, half_of(h)]
                for e in range(2):
                    grad = flat[pl.ds(b * (ROWS * 8) + 2 * ip + e, ROWS, stride=8), :]
                    total = total + grad * s1[2 * ip + e, h, r, :].astype(F32)
                    section[ip, r, half_of(e)] = (grad * gate).astype(BF16)
                gfirst[r, half_of(h)] = total
                return 0

            lax.fori_loop(0, blocks, rows, 0)
            gr[...] += dot(section[ip], x_pair(h, ip), (1, 1))
            return 0

        lax.fori_loop(0, 4, per_pair, 0)

    def grad_of_inputs(h):
        def per_pair(ip, _):
            prod[...] = dot(right_t[...], section[ip], (1, 0))
            for e in range(2):
                giv[2 * ip + e, :, half_of(h)] = prod[:, half_of(e)].astype(BF16)
            return 0

        lax.fori_loop(0, 4, per_pair, 0)

    def to_peers(count, me, src, dst, send_sem, recv_sem, device):
        pltpu.make_async_copy(src.at[me], dst.at[me], recv_sem).start()
        for t in range(1, count):
            d = (me + t) % count
            pltpu.make_async_remote_copy(
                src_ref=src.at[d], dst_ref=dst.at[me], send_sem=send_sem, recv_sem=recv_sem,
                device_id=device(d), device_id_type=MESH,
            ).start()

    def at_ch(d):
        return (s, d)

    def at_y(d):
        return ((d * zs + own_z) * 2 + core, ch)

    def at_z(d):
        return ((own_y * zs + d) * 2 + core, ch)

    def core_copies(n):
        return [
            pltpu.make_async_remote_copy(
                src_ref=src.at[n], dst_ref=dst.at[n], send_sem=r_sem.at[n, 2 * q], recv_sem=r_sem.at[n, 2 * q + 1],
                device_id=(s + 1 - 2 * core, ch), device_id_type=MESH,
            )
            for q, (src, dst) in enumerate(((csend, crecv), (cgsend, cgrecv)))
        ]

    def reduce_core(n, matrix, gates):
        def give(p, _):
            r = pl.ds(pl.multiple_of(p * 16 + (1 - core) * 8, 8), 8)
            csend[n, p] = matrix[r, :].astype(BF16)
            cgsend[n, p] = gates[r, :].astype(BF16)
            return 0

        lax.fori_loop(0, pairs, give, 0, unroll=4)
        for copy in core_copies(n):
            copy.start()

    def reduce_ch(n, matrix, gates):
        for copy in core_copies(n):
            copy.wait()

        def take(p, _):
            r = pl.ds(pl.multiple_of(p * 16 + core * 8, 8), 8)
            total = matrix[r, :] + crecv[n, p].astype(F32)
            for c in range(4):
                half[c, pl.ds(pl.multiple_of(p * 8, 8), 8), :] = total[:, c * LANES : (c + 1) * LANES]
            ygsend[n, p // zs, p % zs] = (gates[r, :] + cgrecv[n, p].astype(F32)).astype(BF16)
            return 0

        lax.fori_loop(0, pairs, take, 0, unroll=4)
        for a in range(chs):
            for b in range(2):
                for c in range(4):
                    lanes = slice(c * LANES, (c + 1) * LANES)
                    xsend[n, a, b, :, lanes] = half[c, pl.ds(2 * a + b, pairs, stride=8), :].astype(BF16)
        to_peers(chs, ch, xsend.at[n], xrecv.at[n], r_sem.at[n, 4], r_sem.at[n, 5], at_ch)
        to_peers(ys, own_y, ygsend.at[n], ygrecv.at[n], r_sem.at[n, 6], r_sem.at[n, 7], at_y)

    def reduce_y(n):
        arrived(xrecv.at[n], r_sem.at[n, 5])
        total = xrecv[n, 0].astype(F32)
        for a in range(1, chs):
            total = total + xrecv[n, a].astype(F32)
        for a in range(ys):
            ysend[n, a] = total[:, a * zs : (a + 1) * zs].astype(BF16)
        to_peers(ys, own_y, ysend.at[n], yrecv.at[n], r_sem.at[n, 8], r_sem.at[n, 9], at_y)

    def reduce_z_gates(n):
        arrived(ygrecv.at[n], r_sem.at[n, 7])
        total = ygrecv[n, 0].astype(F32)
        for a in range(1, ys):
            total = total + ygrecv[n, a].astype(F32)
        zgsend[n] = total.astype(BF16)
        to_peers(zs, own_z, zgsend.at[n], zgrecv.at[n], r_sem.at[n, 10], r_sem.at[n, 11], at_z)

    def reduce_z(n):
        arrived(yrecv.at[n], r_sem.at[n, 9])
        total = yrecv[n, 0].astype(F32)
        for a in range(1, ys):
            total = total + yrecv[n, a].astype(F32)
        total = total.reshape(2 * zs, grid)
        for c in range(4):
            thin[c] = total[:, c * LANES : (c + 1) * LANES]
        for p in range(zs):
            for c in range(4):
                zsend[n, p, :, c * LANES : (c + 1) * LANES] = thin[c, pl.ds(p, 2, stride=zs), :].astype(BF16)
        to_peers(zs, own_z, zsend.at[n], zrecv.at[n], r_sem.at[n, 12], r_sem.at[n, 13], at_z)

    def finish(n, matrix_out, gates_out):
        arrived(zgrecv.at[n], r_sem.at[n, 11])
        gates_out[...] = jnp.sum(zgrecv[n].astype(F32), axis=0)
        arrived(zrecv.at[n], r_sem.at[n, 13])
        matrix_out[...] = jnp.sum(zrecv[n].astype(F32), axis=0)
        for buffer, count, sem in (
            (xsend, chs, 4), (ygsend, ys, 6), (ysend, ys, 8), (zgsend, zs, 10), (zsend, zs, 12)
        ):
            arrived(buffer.at[n, pl.ds(0, count - 1)], r_sem.at[n, sem])

    first_stage(0)
    pl.semaphore_wait(barrier, seqs + chs - 2)
    exchange(0, fsend, frecv, fs_sem, fr_sem)
    first_stage(1)
    exchange(1, fsend, frecv, fs_sem, fr_sem)
    for load in loads[3:]:
        load.wait()
    right_t[...] = right[...].T
    left_t[...] = left[...].T
    gl[...] = jnp.zeros(gl.shape, F32)
    gr[...] = jnp.zeros(gr.shape, F32)
    for h in range(2):
        middle(h)
        exchange(h, bsend, brecv, bs_sem, br_sem)
        if h == 1:
            reduce_core(0, gl, gsecond)
        write_out(h)
    reduce_ch(0, gl, gsecond)
    reduce_y(0)
    last_stage(0)
    grad_of_inputs(0)
    last_stage(1)
    reduce_core(1, gr, gfirst)
    reduce_z_gates(0)
    reduce_z(0)
    grad_of_inputs(1)
    reduce_ch(1, gr, gfirst)
    reduce_z_gates(1)
    reduce_y(1)
    reduce_z(1)
    finish(0, gl_out, gs_out)
    finish(1, gr_out, gf_out)
    for h in range(2):
        arrived(fsend.at[h, pl.ds(0, seqs - 1)], fs_sem.at[h])
        arrived(bsend.at[h, pl.ds(0, seqs - 1)], bs_sem.at[h])


def place(*refs):
    count = len(refs) // 2
    sems = refs[-1]
    copies = [pltpu.make_async_copy(refs[q], refs[count + q], sems.at[q]) for q in range(count)]
    for copy in copies:
        copy.start()
    for copy in copies:
        copy.wait()


def per_device(seqs, zs, chs, inputs, cotangent, right_weight, left_weight, first_gate, second_gate):
    rows, grid, width = inputs.shape
    any_space = pl.BlockSpec(memory_space=pl.ANY)
    hbm = pl.BlockSpec(memory_space=pltpu.HBM)
    vmem = pl.BlockSpec(memory_space=pltpu.VMEM)
    pairs, ys = seqs // 2, seqs // (2 * zs)
    block = (2, seqs, 8, 8, LANES)

    def v(shape, dtype=BF16):
        return pltpu.VMEM(shape, dtype)

    def twice(*shape):
        return [pltpu.VMEM((2,) + shape, BF16)] * 2

    dma = pltpu.SemaphoreType.DMA
    shapes = (
        jax.ShapeDtypeStruct(cotangent.shape, BF16),
        jax.ShapeDtypeStruct(inputs.shape, BF16),
        jax.ShapeDtypeStruct((2, grid), F32),
        jax.ShapeDtypeStruct((2, grid), F32),
        jax.ShapeDtypeStruct((8, width), F32),
        jax.ShapeDtypeStruct((8, width), F32),
    )
    results = pl.pallas_call(
        functools.partial(fused, seqs, zs, chs, grid),
        out_shape=shapes,
        in_specs=[hbm] * 6,
        out_specs=(vmem,) * 6,
        scratch_shapes=[
            v(inputs.shape), v(cotangent.shape), v((grid, grid)), v((grid, grid)), v((grid, width)), v((grid, width)),
            v((grid, grid)), v((grid, grid)), v((8, 2, grid, LANES)), v((grid * 8, LANES), F32), v((grid * 8, LANES), F32),
            v((grid, 2 * LANES), F32), v((grid, 2 * LANES)), v((grid, 2 * LANES)), v((4, grid, 2 * LANES)),
            v((grid, grid), F32), v((grid, grid), F32), v((grid, width), F32), v((grid, width), F32),
            v(block), v(block), v(block), v(block),
            *twice(pairs, 8, grid), *twice(pairs, 8, width),
            v((4, pairs * 8, LANES), F32), *twice(chs, 2, pairs, grid),
            *twice(ys, 2, zs, grid), *twice(ys, zs, 8, width),
            v((4, 2 * zs, LANES), F32), *twice(zs, 2, grid), *twice(zs, 8, width),
            dma((6,)), dma((2,)), dma((2,)), dma((2,)), dma((2,)), dma((2, 14)),
        ],
        compiler_params=pltpu.CompilerParams(
            collective_id=0, has_side_effects=True, vmem_limit_bytes=LIMIT_MIB * 1024 * 1024
        ),
    )(*(
        pltpu.with_memory_space_constraint(array, pltpu.HBM)
        for array in (inputs, cotangent, right_weight, left_weight, first_gate, second_gate)
    ))
    return pl.pallas_call(
        place,
        out_shape=shapes,
        in_specs=[any_space] * 6,
        out_specs=(hbm,) * 6,
        scratch_shapes=[dma((6,))],
        compiler_params=pltpu.CompilerParams(vmem_limit_bytes=4 * 1024 * 1024),
    )(*results)


def solution(mesh):
    placed = (P("seq", None, "ch"), P(None, "seq", "ch"), P(), P(), P(None, "ch"), P(None, "ch"))
    return jax.shard_map(
        functools.partial(per_device, mesh.shape["seq"], CHIPS_Z, mesh.shape["ch"]),
        mesh=mesh,
        in_specs=placed,
        out_specs=(
            P(None, "seq", "ch"),
            P("seq", None, "ch"),
            P(("seq", "ch"), None),
            P(("seq", "ch"), None),
            P("seq", "ch"),
            P("seq", "ch"),
        ),
        check_vma=False,
    )
```

```python
import functools

import jax
import jax.numpy as jnp
from jax import lax
from jax.experimental import pallas as pl
from jax.experimental.pallas import tpu as pltpu
from jax.sharding import PartitionSpec as P

MESH = pl.DeviceIdType.MESH
F32 = jnp.float32
BF16 = jnp.bfloat16
LANES = 128
ROWS = 64
CHIPS_Z = 8
LIMIT_MIB = 44


def dot(a, b, contract):
    return lax.dot_general(a, b, ((contract[:1], contract[1:]), ((), ())), preferred_element_type=F32)


def fused(
    seqs, zs, chs, grid,
    x_hbm, ct_hbm, right_hbm, left_hbm, gate1_hbm, gate2_hbm,
    ov, giv, gr_out, gl_out, gf_out, gs_out,
    xv, ctv, right, left, gate1, gate2,
    right_t, left_t, gate1_p, s1, flat, flat_out, prod, pair, grad_pair, section, gl, gr, gfirst, gsecond,
    fsend, frecv, bsend, brecv,
    csend, crecv, cgsend, cgrecv, half, xysend, xyrecv, ygsend, ygrecv, thin, zsend, zrecv, zgsend, zgrecv,
    in_sem, fs_sem, fr_sem, bs_sem, br_sem, r_sem,
):
    s, ch = lax.axis_index("seq"), lax.axis_index("ch")
    core = s % 2
    own, own_y, own_z = s // 2, s // (2 * zs), (s // 2) % zs
    ys = seqs // (2 * zs)
    pairs = seqs // 2
    blocks = grid // ROWS

    barrier = pltpu.get_barrier_semaphore()

    def greet(t, _):
        pl.semaphore_signal(barrier, inc=1, device_id=((s + t) % seqs, ch), device_id_type=MESH)
        return 0

    def greet_ch(t, _):
        x, y = (ch + 1 + t // ys) % chs, t % ys
        pl.semaphore_signal(barrier, inc=1, device_id=((y * zs + own_z) * 2 + core, x), device_id_type=MESH)
        return 0

    loads = [
        pltpu.make_async_copy(src, dst, in_sem.at[n])
        for n, (src, dst) in enumerate(
            ((x_hbm, xv), (right_hbm, right), (gate1_hbm, gate1), (ct_hbm, ctv), (left_hbm, left), (gate2_hbm, gate2))
        )
    ]
    for load in loads:
        load.start()
    lax.fori_loop(1, seqs, greet, 0)
    lax.fori_loop(0, (chs - 1) * ys, greet_ch, 0)
    for load in loads[:3]:
        load.wait()

    def half_of(h):
        return slice(h * LANES, (h + 1) * LANES)

    def x_pair(h, ip):
        return jnp.concatenate([xv[2 * ip, :, half_of(h)], xv[2 * ip + 1, :, half_of(h)]], axis=1)

    def turn(n, extent):
        odd = n % 2
        return (odd * ((n + 1) // 2) + (1 - odd) * (extent - n // 2)) % extent

    def far_first(t):
        z = (own_z + turn(t % zs, zs)) % zs
        y = (own_y + turn(t // zs % ys, ys)) % ys
        return (y * zs + z) * 2 + (core + t // (zs * ys)) % 2

    def spread(h):
        pltpu.make_async_copy(fsend.at[h, s], frecv.at[h, s], fr_sem.at[h]).start()

        def send(t, _):
            d = far_first(seqs - t)
            pltpu.make_async_remote_copy(
                src_ref=fsend.at[h, d], dst_ref=frecv.at[h, s], send_sem=fs_sem.at[h], recv_sem=fr_sem.at[h],
                device_id=(d, ch), device_id_type=MESH,
            ).start()
            return 0

        lax.fori_loop(1, seqs, send, 0)

    def send_back(h):
        pltpu.make_async_copy(bsend.at[h, s], brecv.at[h, core, own], br_sem.at[h, 1]).start()
        for rel, first, last in ((0, 1, pairs + 1), (1, pairs + 1, seqs)):

            def send(t, _):
                d = far_first(seqs - t)
                pltpu.make_async_remote_copy(
                    src_ref=bsend.at[h, d], dst_ref=brecv.at[h, core, own],
                    send_sem=bs_sem.at[h], recv_sem=br_sem.at[h, rel],
                    device_id=(d, ch), device_id_type=MESH,
                ).start()
                return 0

            lax.fori_loop(first, last, send, 0)

    def arrived(dst, sem):
        pltpu.make_async_copy(dst, dst, sem).wait()

    def first_stage(h):
        def per_pair(ip, _):
            prod[...] = dot(right[...], x_pair(h, ip), (1, 0))

            def rows(b, _):
                r = pl.ds(pl.multiple_of(b * ROWS, ROWS), ROWS)
                gate = gate1[r, half_of(h)].astype(F32)
                for e in range(2):
                    rounded = prod[r, half_of(e)].astype(BF16).astype(F32)
                    flat[pl.ds(b * (ROWS * 8) + 2 * ip + e, ROWS, stride=8), :] = rounded * gate
                    rounded = rounded.reshape(ROWS // 16, 2, 8, LANES)
                    to = pl.ds(pl.multiple_of(b * (ROWS // 2), ROWS // 2), ROWS // 2)
                    for p in range(2):
                        s1[2 * ip + e, h, p, to, :] = rounded[:, p].reshape(ROWS // 2, LANES).astype(BF16)
                return 0

            lax.fori_loop(0, blocks, rows, 0)
            return 0

        lax.fori_loop(0, 4, per_pair, 0)

        def pack(d, _):
            rows = flat[pl.ds(pl.multiple_of(d * 64, 64), 64), :]
            fsend[h, d] = rows.reshape(8, 8, LANES).astype(BF16)
            return 0

        lax.fori_loop(0, seqs, pack, 0, unroll=4)

    def middle(h):
        def unpack(b, _):
            m = pl.ds(pl.multiple_of(b * 8, 8), 8)
            flat[pl.ds(pl.multiple_of(b * 64, 64), 64), :] = ctv[m, :, half_of(h)].astype(F32).reshape(64, LANES)
            return 0

        lax.fori_loop(0, grid // 8, unpack, 0, unroll=4)
        gsecond[:, half_of(h)] = jnp.zeros((grid, LANES), F32)
        arrived(frecv.at[h], fr_sem.at[h])

        def per_pair(kp, _):
            pair[...] = jnp.concatenate(
                [frecv[h, :, 2 * kp + e].astype(F32).reshape(grid, LANES).astype(BF16) for e in range(2)], axis=1
            )
            prod[...] = dot(left[...], pair[...], (1, 0))

            def rows(b, _):
                r = pl.ds(pl.multiple_of(b * ROWS, ROWS), ROWS)
                gate = gate2[r, half_of(h)].astype(F32)
                total = gsecond[r, half_of(h)]
                for e in range(2):
                    at = pl.ds(b * (ROWS * 8) + 2 * kp + e, ROWS, stride=8)
                    mixed = prod[r, half_of(e)]
                    grad_out = flat[at, :]
                    logistic = 1.0 / (1.0 + jnp.exp(-mixed))
                    activated = mixed * logistic
                    flat_out[at, :] = activated * gate
                    total = total + grad_out * activated
                    grad_mixed = grad_out * gate * logistic * (1.0 + mixed * (1.0 - logistic))
                    grad_pair[r, half_of(e)] = grad_mixed.astype(BF16)
                gsecond[r, half_of(h)] = total
                return 0

            lax.fori_loop(0, blocks, rows, 0)
            gl[...] += dot(grad_pair[...], pair[...], (1, 1))
            prod[...] = dot(left_t[...], grad_pair[...], (1, 0))
            for e in range(2):
                bsend[h, :, 2 * kp + e] = prod[:, half_of(e)].reshape(seqs, 8, LANES).astype(BF16)
            return 0

        lax.fori_loop(0, 4, per_pair, 0)

    def write_out(h):
        def pack(b, _):
            m = pl.ds(pl.multiple_of(b * 8, 8), 8)
            rows = flat_out[pl.ds(pl.multiple_of(b * 64, 64), 64), :]
            ov[m, :, half_of(h)] = rows.reshape(8, 8, LANES).astype(BF16)
            return 0

        lax.fori_loop(0, grid // 8, pack, 0, unroll=4)

    def parity(rel):
        return core if rel else 1 - core

    def last_stage(h, rel):
        p = parity(rel)
        arrived(brecv.at[h, p], br_sem.at[h, rel])

        def unpack(b, _):
            rows = brecv[h, p, b].astype(F32).reshape(64, LANES)
            flat[pl.ds(pl.multiple_of(b * 64, 64), 64), :] = rows
            return 0

        lax.fori_loop(0, pairs, unpack, 0, unroll=4)

        def per_pair(ip, _):
            def rows(b, _):
                r = pl.ds(pl.multiple_of(b * ROWS, ROWS), ROWS)
                gate = gate1_p[p, r, half_of(h)]
                total = gfirst[p, r, half_of(h)]
                for e in range(2):
                    grad = flat[pl.ds(b * (ROWS * 8) + 2 * ip + e, ROWS, stride=8), :]
                    total = total + grad * s1[2 * ip + e, h, p, r, :].astype(F32)
                    section[p, ip, r, half_of(e)] = (grad * gate).astype(BF16)
                gfirst[p, r, half_of(h)] = total
                return 0

            lax.fori_loop(0, blocks // 2, rows, 0)
            gr[p] += dot(section[p, ip], x_pair(h, ip), (1, 1))
            return 0

        lax.fori_loop(0, 4, per_pair, 0)

    def grad_of_inputs(h):
        def per_pair(ip, _):
            prod[...] = dot(right_t[0], section[0, ip], (1, 0)) + dot(right_t[1], section[1, ip], (1, 0))
            for e in range(2):
                giv[2 * ip + e, :, half_of(h)] = prod[:, half_of(e)].astype(BF16)
            return 0

        lax.fori_loop(0, 4, per_pair, 0)

    def to_peers(count, me, src, dst, send_sem, recv_sem, device):
        pltpu.make_async_copy(src.at[me], dst.at[me], recv_sem).start()
        for t in range(1, count):
            d = (me + t) % count
            pltpu.make_async_remote_copy(
                src_ref=src.at[d], dst_ref=dst.at[me], send_sem=send_sem, recv_sem=recv_sem,
                device_id=device(d), device_id_type=MESH,
            ).start()

    def at_xy(d):
        return ((d % ys * zs + own_z) * 2 + core, d // ys)

    def at_y(d):
        return ((d * zs + own_z) * 2 + core, ch)

    def at_z(d):
        return ((own_y * zs + d) * 2 + core, ch)

    def core_copies(n):
        return [
            pltpu.make_async_remote_copy(
                src_ref=src.at[n], dst_ref=dst.at[n], send_sem=r_sem.at[n, 2 * q], recv_sem=r_sem.at[n, 2 * q + 1],
                device_id=(s + 1 - 2 * core, ch), device_id_type=MESH,
            )
            for q, (src, dst) in enumerate(((csend, crecv), (cgsend, cgrecv)))
        ]

    def reduce_core(n, rows):
        def give(q, _):
            csend[n, q], cgsend[n, q] = (part.astype(BF16) for part in rows(1 - core, q))
            return 0

        lax.fori_loop(0, pairs, give, 0, unroll=4)
        for copy in core_copies(n):
            copy.start()

    def reduce_xy(n, rows):
        for copy in core_copies(n):
            copy.wait()

        def take(q, _):
            matrix, gates = rows(core, q)
            total = matrix + crecv[n, q].astype(F32)
            for c in range(4):
                half[c, pl.ds(pl.multiple_of(q * 8, 8), 8), :] = total[:, c * LANES : (c + 1) * LANES]
            ygsend[n, q // zs, q % zs] = (gates + cgrecv[n, q].astype(F32)).astype(BF16)
            return 0

        lax.fori_loop(0, pairs, take, 0, unroll=4)
        for a in range(chs):
            for b in range(2):
                for c in range(4):
                    lanes = slice(c * LANES, (c + 1) * LANES)
                    part = half[c, pl.ds(2 * a + b, pairs, stride=8), :]
                    for y in range(ys):
                        xysend[n, a * ys + y, b, :, lanes] = part[y * zs : (y + 1) * zs].astype(BF16)
        to_peers(chs * ys, ch * ys + own_y, xysend.at[n], xyrecv.at[n], r_sem.at[n, 4], r_sem.at[n, 5], at_xy)
        to_peers(ys, own_y, ygsend.at[n], ygrecv.at[n], r_sem.at[n, 6], r_sem.at[n, 7], at_y)

    def reduce_z_gates(n):
        arrived(ygrecv.at[n], r_sem.at[n, 7])
        total = ygrecv[n, 0].astype(F32)
        for a in range(1, ys):
            total = total + ygrecv[n, a].astype(F32)
        zgsend[n] = total.astype(BF16)
        to_peers(zs, own_z, zgsend.at[n], zgrecv.at[n], r_sem.at[n, 8], r_sem.at[n, 9], at_z)

    def reduce_z(n):
        arrived(xyrecv.at[n], r_sem.at[n, 5])
        total = xyrecv[n, 0].astype(F32)
        for a in range(1, chs * ys):
            total = total + xyrecv[n, a].astype(F32)
        total = total.reshape(2 * zs, grid)
        for c in range(4):
            thin[c] = total[:, c * LANES : (c + 1) * LANES]
        for p in range(zs):
            for c in range(4):
                zsend[n, p, :, c * LANES : (c + 1) * LANES] = thin[c, pl.ds(p, 2, stride=zs), :].astype(BF16)
        to_peers(zs, own_z, zsend.at[n], zrecv.at[n], r_sem.at[n, 10], r_sem.at[n, 11], at_z)

    def finish(n, matrix_out, gates_out):
        arrived(zgrecv.at[n], r_sem.at[n, 9])
        gates_out[...] = jnp.sum(zgrecv[n].astype(F32), axis=0)
        arrived(zrecv.at[n], r_sem.at[n, 11])
        matrix_out[...] = jnp.sum(zrecv[n].astype(F32), axis=0)
        for buffer, count, sem in (
            (xysend, chs * ys, 4), (ygsend, ys, 6), (zgsend, zs, 8), (zsend, zs, 10)
        ):
            arrived(buffer.at[n, pl.ds(0, count - 1)], r_sem.at[n, sem])

    def left_rows(p, q):
        r = pl.ds(pl.multiple_of(q * 16 + p * 8, 8), 8)
        return gl[r, :], gsecond[r, :]

    def right_rows_of(p, q):
        r = pl.ds(pl.multiple_of(q * 8, 8), 8)
        return gr[p, r, :], gfirst[p, r, :]

    first_stage(0)
    pl.semaphore_wait(barrier, seqs - 1 + (chs - 1) * ys)
    spread(0)
    first_stage(1)
    spread(1)
    for load in loads[3:]:
        load.wait()
    right_rows = right[...].astype(F32).reshape(pairs, 2, 8, grid)
    for p in range(2):
        right_t[p] = right_rows[:, p].reshape(grid // 2, grid).astype(BF16).T

    def split_gate(q, _):
        rows = gate1[pl.ds(pl.multiple_of(q * 16, 16), 16), :].astype(F32)
        for p in range(2):
            gate1_p[p, pl.ds(pl.multiple_of(q * 8, 8), 8), :] = rows[p * 8 : p * 8 + 8]
        return 0

    lax.fori_loop(0, pairs, split_gate, 0)
    gfirst[...] = jnp.zeros(gfirst.shape, F32)
    left_t[...] = left[...].T
    gl[...] = jnp.zeros(gl.shape, F32)
    gr[...] = jnp.zeros(gr.shape, F32)
    for h in range(2):
        middle(h)
        send_back(h)
        if h == 1:
            reduce_core(0, left_rows)
        write_out(h)
    reduce_xy(0, left_rows)
    last_stage(0, 0)
    last_stage(0, 1)
    grad_of_inputs(0)
    last_stage(1, 0)
    reduce_core(1, right_rows_of)
    reduce_z_gates(0)
    reduce_z(0)
    last_stage(1, 1)
    reduce_xy(1, right_rows_of)
    grad_of_inputs(1)
    reduce_z_gates(1)
    reduce_z(1)
    finish(0, gl_out, gs_out)
    finish(1, gr_out, gf_out)
    for h in range(2):
        arrived(fsend.at[h, pl.ds(0, seqs - 1)], fs_sem.at[h])
        arrived(bsend.at[h, pl.ds(0, seqs - 1)], bs_sem.at[h])


def place(*refs):
    count = len(refs) // 2
    sems = refs[-1]
    copies = [pltpu.make_async_copy(refs[q], refs[count + q], sems.at[q]) for q in range(count)]
    for copy in copies:
        copy.start()
    for copy in copies:
        copy.wait()


def per_device(seqs, zs, chs, inputs, cotangent, right_weight, left_weight, first_gate, second_gate):
    rows, grid, width = inputs.shape
    any_space = pl.BlockSpec(memory_space=pl.ANY)
    hbm = pl.BlockSpec(memory_space=pltpu.HBM)
    vmem = pl.BlockSpec(memory_space=pltpu.VMEM)
    pairs, ys = seqs // 2, seqs // (2 * zs)
    block = (2, seqs, 8, 8, LANES)

    def v(shape, dtype=BF16):
        return pltpu.VMEM(shape, dtype)

    def twice(*shape):
        return [pltpu.VMEM((2,) + shape, BF16)] * 2

    dma = pltpu.SemaphoreType.DMA
    shapes = (
        jax.ShapeDtypeStruct(cotangent.shape, BF16),
        jax.ShapeDtypeStruct(inputs.shape, BF16),
        jax.ShapeDtypeStruct((2, grid), F32),
        jax.ShapeDtypeStruct((2, grid), F32),
        jax.ShapeDtypeStruct((8, width), F32),
        jax.ShapeDtypeStruct((8, width), F32),
    )
    results = pl.pallas_call(
        functools.partial(fused, seqs, zs, chs, grid),
        out_shape=shapes,
        in_specs=[hbm] * 6,
        out_specs=(vmem,) * 6,
        scratch_shapes=[
            v(inputs.shape), v(cotangent.shape), v((grid, grid)), v((grid, grid)), v((grid, width)), v((grid, width)),
            v((2, grid, grid // 2)), v((grid, grid)), v((2, grid // 2, width), F32), v((8, 2, 2, grid // 2, LANES)), v((grid * 8, LANES), F32), v((grid * 8, LANES), F32),
            v((grid, 2 * LANES), F32), v((grid, 2 * LANES)), v((grid, 2 * LANES)), v((2, 4, grid // 2, 2 * LANES)),
            v((grid, grid), F32), v((2, grid // 2, grid), F32), v((2, grid // 2, width), F32), v((grid, width), F32),
            v(block), v(block), v(block), v((2, 2, pairs, 8, 8, LANES)),
            *twice(pairs, 8, grid), *twice(pairs, 8, width),
            v((4, pairs * 8, LANES), F32), *twice(chs * ys, 2, zs, grid),
            *twice(ys, zs, 8, width),
            v((4, 2 * zs, LANES), F32), *twice(zs, 2, grid), *twice(zs, 8, width),
            dma((6,)), dma((2,)), dma((2,)), dma((2,)), dma((2, 2)), dma((2, 12)),
        ],
        compiler_params=pltpu.CompilerParams(
            collective_id=0, has_side_effects=True, vmem_limit_bytes=LIMIT_MIB * 1024 * 1024
        ),
    )(*(
        pltpu.with_memory_space_constraint(array, pltpu.HBM)
        for array in (inputs, cotangent, right_weight, left_weight, first_gate, second_gate)
    ))
    return pl.pallas_call(
        place,
        out_shape=shapes,
        in_specs=[any_space] * 6,
        out_specs=(hbm,) * 6,
        scratch_shapes=[dma((6,))],
        compiler_params=pltpu.CompilerParams(vmem_limit_bytes=4 * 1024 * 1024),
    )(*results)


def solution(mesh):
    placed = (P("seq", None, "ch"), P(None, "seq", "ch"), P(), P(), P(None, "ch"), P(None, "ch"))
    return jax.shard_map(
        functools.partial(per_device, mesh.shape["seq"], CHIPS_Z, mesh.shape["ch"]),
        mesh=mesh,
        in_specs=placed,
        out_specs=(
            P(None, "seq", "ch"),
            P("seq", None, "ch"),
            P(("seq", "ch"), None),
            P(("seq", "ch"), None),
            P("seq", "ch"),
            P("seq", "ch"),
        ),
        check_vma=False,
    )
```

```python
import functools

import jax
import jax.numpy as jnp
from jax import lax
from jax.experimental import pallas as pl
from jax.experimental.pallas import tpu as pltpu
from jax.sharding import PartitionSpec as P

MESH = pl.DeviceIdType.MESH
F32 = jnp.float32
BF16 = jnp.bfloat16
LANES = 128
ROWS = 64
CHIPS_Z = 8
LIMIT_MIB = 44


def dot(a, b, contract):
    return lax.dot_general(a, b, ((contract[:1], contract[1:]), ((), ())), preferred_element_type=F32)


def fused(
    seqs, zs, chs, grid,
    x_hbm, ct_hbm, right_hbm, left_hbm, gate1_hbm, gate2_hbm,
    ov, giv, gr_out, gl_out, gf_out, gs_out,
    xv, ctv, right, left, gate1, gate2,
    right_t, left_t, gate1_p, s1, flat, flat_out, prod, pair, grad_pair, section, gl, gr, gfirst, gsecond,
    fsend, frecv, bsend, brecv,
    csend, crecv, cgsend, cgrecv, half, xysend, xyrecv, ygsend, ygrecv, thin, zsend, zrecv, zgsend, zgrecv,
    in_sem, fs_sem, fr_sem, bs_sem, br_sem, r_sem,
):
    s, ch = lax.axis_index("seq"), lax.axis_index("ch")
    core = s % 2
    own, own_y, own_z = s // 2, s // (2 * zs), (s // 2) % zs
    ys = seqs // (2 * zs)
    pairs = seqs // 2
    blocks = grid // ROWS

    barrier = pltpu.get_barrier_semaphore()

    def turn(n, extent):
        odd = n % 2
        return (odd * ((n + 1) // 2) + (1 - odd) * (extent - n // 2)) % extent

    def far_first(t):
        z = (own_z + turn(t % zs, zs)) % zs
        y = (own_y + turn(t // zs % ys, ys)) % ys
        return (y * zs + z) * 2 + (core + t // (zs * ys)) % 2

    def greet(t, _):
        pl.semaphore_signal(barrier, inc=1, device_id=(far_first(seqs - t), ch), device_id_type=MESH)
        return 0

    def greet_ch(t, _):
        x, y = (ch + 1 + t // ys) % chs, t % ys
        pl.semaphore_signal(barrier, inc=1, device_id=((y * zs + own_z) * 2 + core, x), device_id_type=MESH)
        return 0

    loads = [
        pltpu.make_async_copy(src, dst, in_sem.at[n])
        for n, (src, dst) in enumerate(
            ((x_hbm, xv), (right_hbm, right), (gate1_hbm, gate1), (ct_hbm, ctv), (left_hbm, left), (gate2_hbm, gate2))
        )
    ]
    for load in loads[:3]:
        load.start()
    lax.fori_loop(1, seqs, greet, 0)
    lax.fori_loop(0, (chs - 1) * ys, greet_ch, 0)
    for load in loads[3:]:
        load.start()
    for load in loads[:3]:
        load.wait()

    def half_of(h):
        return slice(h * LANES, (h + 1) * LANES)

    def x_pair(h, ip):
        return jnp.concatenate([xv[2 * ip, :, half_of(h)], xv[2 * ip + 1, :, half_of(h)]], axis=1)

    def spread(h):
        pltpu.make_async_copy(fsend.at[h, s], frecv.at[h, s], fr_sem.at[h]).start()

        def send(t, _):
            d = far_first(seqs - t)
            pltpu.make_async_remote_copy(
                src_ref=fsend.at[h, d], dst_ref=frecv.at[h, s], send_sem=fs_sem.at[h], recv_sem=fr_sem.at[h],
                device_id=(d, ch), device_id_type=MESH,
            ).start()
            return 0

        lax.fori_loop(1, seqs, send, 0)

    def send_back(h):
        pltpu.make_async_copy(bsend.at[h, s], brecv.at[h, core, own], br_sem.at[h, ys]).start()
        for part, first, last in [(0, 1, pairs + 1)] + [
            (v + 1, pairs + 1 + v * zs, min(pairs + 1 + (v + 1) * zs, seqs)) for v in range(ys)
        ]:

            def send(t, _):
                d = far_first(seqs - t)
                pltpu.make_async_remote_copy(
                    src_ref=bsend.at[h, d], dst_ref=brecv.at[h, core, own],
                    send_sem=bs_sem.at[h], recv_sem=br_sem.at[h, part],
                    device_id=(d, ch), device_id_type=MESH,
                ).start()
                return 0

            lax.fori_loop(first, last, send, 0)

    def arrived(dst, sem):
        pltpu.make_async_copy(dst, dst, sem).wait()

    def first_stage(h):
        def per_pair(ip, _):
            prod[...] = dot(right[...], x_pair(h, ip), (1, 0))

            def rows(b, _):
                r = pl.ds(pl.multiple_of(b * ROWS, ROWS), ROWS)
                gate = gate1[r, half_of(h)].astype(F32)
                for e in range(2):
                    rounded = prod[r, half_of(e)].astype(BF16).astype(F32)
                    flat[pl.ds(b * (ROWS * 8) + 2 * ip + e, ROWS, stride=8), :] = rounded * gate
                    rounded = rounded.reshape(ROWS // 16, 2, 8, LANES)
                    to = pl.ds(pl.multiple_of(b * (ROWS // 2), ROWS // 2), ROWS // 2)
                    for p in range(2):
                        s1[2 * ip + e, h, p, to, :] = rounded[:, p].reshape(ROWS // 2, LANES).astype(BF16)
                return 0

            lax.fori_loop(0, blocks, rows, 0)
            return 0

        lax.fori_loop(0, 4, per_pair, 0)

        def pack(d, _):
            rows = flat[pl.ds(pl.multiple_of(d * 64, 64), 64), :]
            fsend[h, d] = rows.reshape(8, 8, LANES).astype(BF16)
            return 0

        lax.fori_loop(0, seqs, pack, 0, unroll=4)

    def middle(h):
        def unpack(b, _):
            m = pl.ds(pl.multiple_of(b * 8, 8), 8)
            flat[pl.ds(pl.multiple_of(b * 64, 64), 64), :] = ctv[m, :, half_of(h)].astype(F32).reshape(64, LANES)
            return 0

        lax.fori_loop(0, grid // 8, unpack, 0, unroll=4)
        gsecond[:, half_of(h)] = jnp.zeros((grid, LANES), F32)
        arrived(frecv.at[h], fr_sem.at[h])

        def per_pair(kp, _):
            pair[...] = jnp.concatenate(
                [frecv[h, :, 2 * kp + e].astype(F32).reshape(grid, LANES).astype(BF16) for e in range(2)], axis=1
            )
            prod[...] = dot(left[...], pair[...], (1, 0))

            def rows(b, _):
                r = pl.ds(pl.multiple_of(b * ROWS, ROWS), ROWS)
                gate = gate2[r, half_of(h)].astype(F32)
                total = gsecond[r, half_of(h)]
                for e in range(2):
                    at = pl.ds(b * (ROWS * 8) + 2 * kp + e, ROWS, stride=8)
                    mixed = prod[r, half_of(e)]
                    grad_out = flat[at, :]
                    logistic = 1.0 / (1.0 + jnp.exp(-mixed))
                    activated = mixed * logistic
                    flat_out[at, :] = activated * gate
                    total = total + grad_out * activated
                    grad_mixed = grad_out * gate * logistic * (1.0 + mixed * (1.0 - logistic))
                    grad_pair[r, half_of(e)] = grad_mixed.astype(BF16)
                gsecond[r, half_of(h)] = total
                return 0

            lax.fori_loop(0, blocks, rows, 0)
            gl[...] += dot(grad_pair[...], pair[...], (1, 1))
            prod[...] = dot(left_t[...], grad_pair[...], (1, 0))
            for e in range(2):
                bsend[h, :, 2 * kp + e] = prod[:, half_of(e)].reshape(seqs, 8, LANES).astype(BF16)
            return 0

        lax.fori_loop(0, 4, per_pair, 0)

    def write_out(h):
        def pack(b, _):
            m = pl.ds(pl.multiple_of(b * 8, 8), 8)
            rows = flat_out[pl.ds(pl.multiple_of(b * 64, 64), 64), :]
            ov[m, :, half_of(h)] = rows.reshape(8, 8, LANES).astype(BF16)
            return 0

        lax.fori_loop(0, grid // 8, pack, 0, unroll=4)

    def y_of_part(part):
        return (own_y + ys - turn(ys - part, ys)) % ys

    def rows_arrived(h, part):
        if part == 0:
            arrived(brecv.at[h, 1 - core], br_sem.at[h, 0])
        else:
            y = y_of_part(part)
            arrived(brecv.at[h, core, pl.ds(y * zs, zs)], br_sem.at[h, part])

    def last_stage(h, p, y, count):
        def unpack(b, _):
            rows = brecv[h, p, y * zs + b].astype(F32).reshape(64, LANES)
            flat[pl.ds(pl.multiple_of(b * 64, 64), 64), :] = rows
            return 0

        lax.fori_loop(0, count * zs, unpack, 0, unroll=4)
        whole = pl.ds(pl.multiple_of(y * ROWS, ROWS), count * ROWS)

        def per_pair(ip, _):
            def rows(b, _):
                r = pl.ds(pl.multiple_of((y + b) * ROWS, ROWS), ROWS)
                gate = gate1_p[p, r, half_of(h)]
                total = gfirst[p, r, half_of(h)]
                for e in range(2):
                    grad = flat[pl.ds(b * (ROWS * 8) + 2 * ip + e, ROWS, stride=8), :]
                    total = total + grad * s1[2 * ip + e, h, p, r, :].astype(F32)
                    section[p, ip, r, half_of(e)] = (grad * gate).astype(BF16)
                gfirst[p, r, half_of(h)] = total
                return 0

            lax.fori_loop(0, count, rows, 0)
            gr[p, whole, :] += dot(section[p, ip, whole, :], x_pair(h, ip), (1, 1))
            return 0

        lax.fori_loop(0, 4, per_pair, 0)

    def grad_of_inputs(h):
        def per_pair(ip, _):
            prod[...] = dot(right_t[0], section[0, ip], (1, 0)) + dot(right_t[1], section[1, ip], (1, 0))
            for e in range(2):
                giv[2 * ip + e, :, half_of(h)] = prod[:, half_of(e)].astype(BF16)
            return 0

        lax.fori_loop(0, 4, per_pair, 0)

    def to_peers(count, me, src, dst, send_sem, recv_sem, device):
        pltpu.make_async_copy(src.at[me], dst.at[me], recv_sem).start()
        for t in range(1, count):
            d = (me + t) % count
            pltpu.make_async_remote_copy(
                src_ref=src.at[d], dst_ref=dst.at[me], send_sem=send_sem, recv_sem=recv_sem,
                device_id=device(d), device_id_type=MESH,
            ).start()

    def at_z(d):
        return ((own_y * zs + d) * 2 + core, ch)

    def core_copies(n):
        return [
            pltpu.make_async_remote_copy(
                src_ref=src.at[n], dst_ref=dst.at[n], send_sem=r_sem.at[n, 2 * q], recv_sem=r_sem.at[n, 2 * q + 1],
                device_id=(s + 1 - 2 * core, ch), device_id_type=MESH,
            )
            for q, (src, dst) in enumerate(((csend, crecv), (cgsend, cgrecv)))
        ]

    def reduce_core(n, rows):
        def give(q, _):
            csend[n, q], cgsend[n, q] = (part.astype(BF16) for part in rows(1 - core, q))
            return 0

        lax.fori_loop(0, pairs, give, 0, unroll=4)
        for copy in core_copies(n):
            copy.start()

    def core_arrived(n):
        for copy in core_copies(n):
            copy.wait()

    def reduce_xy(n, rows, y, mine):
        def take(z, _):
            q = y * zs + z
            matrix, gates = rows(core, q)
            total = matrix + crecv[n, q].astype(F32)
            for c in range(4):
                half[c, pl.ds(pl.multiple_of(q * 8, 8), 8), :] = total[:, c * LANES : (c + 1) * LANES]
            ygsend[n, y, z] = (gates + cgrecv[n, q].astype(F32)).astype(BF16)
            return 0

        lax.fori_loop(0, zs, take, 0, unroll=4)
        for a in range(chs):
            for b in range(2):
                for c in range(4):
                    part = half[c, pl.ds(y * (8 * zs) + 2 * a + b, zs, stride=8), :]
                    xysend[n, a * ys + y, b, :, c * LANES : (c + 1) * LANES] = part.astype(BF16)
        to = ch * ys + own_y
        for t in range(chs):
            d = (ch + t) % chs
            if mine and t == 0:
                pltpu.make_async_copy(xysend.at[n, to], xyrecv.at[n, to], r_sem.at[n, 5]).start()
            else:
                pltpu.make_async_remote_copy(
                    src_ref=xysend.at[n, d * ys + y], dst_ref=xyrecv.at[n, to],
                    send_sem=r_sem.at[n, 4], recv_sem=r_sem.at[n, 5],
                    device_id=((y * zs + own_z) * 2 + core, d), device_id_type=MESH,
                ).start()
        if mine:
            pltpu.make_async_copy(ygsend.at[n, y], ygrecv.at[n, y], r_sem.at[n, 7]).start()
        else:
            pltpu.make_async_remote_copy(
                src_ref=ygsend.at[n, y], dst_ref=ygrecv.at[n, own_y], send_sem=r_sem.at[n, 6], recv_sem=r_sem.at[n, 7],
                device_id=((y * zs + own_z) * 2 + core, ch), device_id_type=MESH,
            ).start()

    def reduce_z_gates(n):
        arrived(ygrecv.at[n], r_sem.at[n, 7])
        total = ygrecv[n, 0].astype(F32)
        for a in range(1, ys):
            total = total + ygrecv[n, a].astype(F32)
        zgsend[n] = total.astype(BF16)
        to_peers(zs, own_z, zgsend.at[n], zgrecv.at[n], r_sem.at[n, 8], r_sem.at[n, 9], at_z)

    def reduce_z(n):
        arrived(xyrecv.at[n], r_sem.at[n, 5])
        total = xyrecv[n, 0].astype(F32)
        for a in range(1, chs * ys):
            total = total + xyrecv[n, a].astype(F32)
        total = total.reshape(2 * zs, grid)
        for c in range(4):
            thin[c] = total[:, c * LANES : (c + 1) * LANES]
        for p in range(zs):
            for c in range(4):
                zsend[n, p, :, c * LANES : (c + 1) * LANES] = thin[c, pl.ds(p, 2, stride=zs), :].astype(BF16)
        to_peers(zs, own_z, zsend.at[n], zrecv.at[n], r_sem.at[n, 10], r_sem.at[n, 11], at_z)

    def finish(n, matrix_out, gates_out):
        arrived(zgrecv.at[n], r_sem.at[n, 9])
        gates_out[...] = jnp.sum(zgrecv[n].astype(F32), axis=0)
        arrived(zrecv.at[n], r_sem.at[n, 11])
        matrix_out[...] = jnp.sum(zrecv[n].astype(F32), axis=0)
        for buffer, count, sem in (
            (xysend, chs * ys, 4), (ygsend, ys, 6), (zgsend, zs, 8), (zsend, zs, 10)
        ):
            arrived(buffer.at[n, pl.ds(0, count - 1)], r_sem.at[n, sem])

    def left_rows(p, q):
        r = pl.ds(pl.multiple_of(q * 16 + p * 8, 8), 8)
        return gl[r, :], gsecond[r, :]

    def right_rows_of(p, q):
        r = pl.ds(pl.multiple_of(q * 8, 8), 8)
        return gr[p, r, :], gfirst[p, r, :]

    first_stage(0)
    pl.semaphore_wait(barrier, seqs - 1 + (chs - 1) * ys)
    spread(0)
    first_stage(1)
    spread(1)
    for load in loads[3:]:
        load.wait()
    right_rows = right[...].astype(F32).reshape(pairs, 2, 8, grid)
    for p in range(2):
        right_t[p] = right_rows[:, p].reshape(grid // 2, grid).astype(BF16).T

    def split_gate(q, _):
        rows = gate1[pl.ds(pl.multiple_of(q * 16, 16), 16), :].astype(F32)
        for p in range(2):
            gate1_p[p, pl.ds(pl.multiple_of(q * 8, 8), 8), :] = rows[p * 8 : p * 8 + 8]
        return 0

    lax.fori_loop(0, pairs, split_gate, 0)
    gfirst[...] = jnp.zeros(gfirst.shape, F32)
    left_t[...] = left[...].T
    gl[...] = jnp.zeros(gl.shape, F32)
    gr[...] = jnp.zeros(gr.shape, F32)
    for h in range(2):
        middle(h)
        send_back(h)
        if h == 1:
            reduce_core(0, left_rows)
        write_out(h)
    core_arrived(0)
    for part in range(1, ys + 1):
        reduce_xy(0, left_rows, y_of_part(part), part == ys)
    rows_arrived(0, 0)
    last_stage(0, 1 - core, 0, ys)
    for part in range(1, ys + 1):
        rows_arrived(0, part)
    last_stage(0, core, 0, ys)
    grad_of_inputs(0)
    rows_arrived(1, 0)
    last_stage(1, 1 - core, 0, ys)
    reduce_core(1, right_rows_of)
    reduce_z_gates(0)
    reduce_z(0)
    core_arrived(1)
    for part in range(1, ys + 1):
        rows_arrived(1, part)
        last_stage(1, core, y_of_part(part), 1)
        reduce_xy(1, right_rows_of, y_of_part(part), part == ys)
    grad_of_inputs(1)
    finish(0, gl_out, gs_out)
    reduce_z_gates(1)
    reduce_z(1)
    finish(1, gr_out, gf_out)
    for h in range(2):
        arrived(fsend.at[h, pl.ds(0, seqs - 1)], fs_sem.at[h])
        arrived(bsend.at[h, pl.ds(0, seqs - 1)], bs_sem.at[h])


def place(*refs):
    count = len(refs) // 2
    sems = refs[-1]
    copies = [pltpu.make_async_copy(refs[q], refs[count + q], sems.at[q]) for q in range(count)]
    for copy in copies:
        copy.start()
    for copy in copies:
        copy.wait()


def per_device(seqs, zs, chs, inputs, cotangent, right_weight, left_weight, first_gate, second_gate):
    rows, grid, width = inputs.shape
    any_space = pl.BlockSpec(memory_space=pl.ANY)
    hbm = pl.BlockSpec(memory_space=pltpu.HBM)
    vmem = pl.BlockSpec(memory_space=pltpu.VMEM)
    pairs, ys = seqs // 2, seqs // (2 * zs)
    block = (2, seqs, 8, 8, LANES)

    def v(shape, dtype=BF16):
        return pltpu.VMEM(shape, dtype)

    def twice(*shape):
        return [pltpu.VMEM((2,) + shape, BF16)] * 2

    dma = pltpu.SemaphoreType.DMA
    shapes = (
        jax.ShapeDtypeStruct(cotangent.shape, BF16),
        jax.ShapeDtypeStruct(inputs.shape, BF16),
        jax.ShapeDtypeStruct((2, grid), F32),
        jax.ShapeDtypeStruct((2, grid), F32),
        jax.ShapeDtypeStruct((8, width), F32),
        jax.ShapeDtypeStruct((8, width), F32),
    )
    results = pl.pallas_call(
        functools.partial(fused, seqs, zs, chs, grid),
        out_shape=shapes,
        in_specs=[hbm] * 6,
        out_specs=(vmem,) * 6,
        scratch_shapes=[
            v(inputs.shape), v(cotangent.shape), v((grid, grid)), v((grid, grid)), v((grid, width)), v((grid, width)),
            v((2, grid, grid // 2)), v((grid, grid)), v((2, grid // 2, width), F32), v((8, 2, 2, grid // 2, LANES)), v((grid * 8, LANES), F32), v((grid * 8, LANES), F32),
            v((grid, 2 * LANES), F32), v((grid, 2 * LANES)), v((grid, 2 * LANES)), v((2, 4, grid // 2, 2 * LANES)),
            v((grid, grid), F32), v((2, grid // 2, grid), F32), v((2, grid // 2, width), F32), v((grid, width), F32),
            v(block), v(block), v(block), v((2, 2, pairs, 8, 8, LANES)),
            *twice(pairs, 8, grid), *twice(pairs, 8, width),
            v((4, pairs * 8, LANES), F32), *twice(chs * ys, 2, zs, grid),
            *twice(ys, zs, 8, width),
            v((4, 2 * zs, LANES), F32), *twice(zs, 2, grid), *twice(zs, 8, width),
            dma((6,)), dma((2,)), dma((2,)), dma((2,)), dma((2, ys + 1)), dma((2, 12)),
        ],
        compiler_params=pltpu.CompilerParams(
            collective_id=0, has_side_effects=True, vmem_limit_bytes=LIMIT_MIB * 1024 * 1024
        ),
    )(*(
        pltpu.with_memory_space_constraint(array, pltpu.HBM)
        for array in (inputs, cotangent, right_weight, left_weight, first_gate, second_gate)
    ))
    return pl.pallas_call(
        place,
        out_shape=shapes,
        in_specs=[any_space] * 6,
        out_specs=(hbm,) * 6,
        scratch_shapes=[dma((6,))],
        compiler_params=pltpu.CompilerParams(vmem_limit_bytes=4 * 1024 * 1024),
    )(*results)


def solution(mesh):
    placed = (P("seq", None, "ch"), P(None, "seq", "ch"), P(), P(), P(None, "ch"), P(None, "ch"))
    return jax.shard_map(
        functools.partial(per_device, mesh.shape["seq"], CHIPS_Z, mesh.shape["ch"]),
        mesh=mesh,
        in_specs=placed,
        out_specs=(
            P(None, "seq", "ch"),
            P("seq", None, "ch"),
            P(("seq", "ch"), None),
            P(("seq", "ch"), None),
            P("seq", "ch"),
            P("seq", "ch"),
        ),
        check_vma=False,
    )
```

```python
import functools

import jax
import jax.numpy as jnp
from jax import lax
from jax.experimental import pallas as pl
from jax.experimental.pallas import tpu as pltpu
from jax.sharding import PartitionSpec as P

MESH = pl.DeviceIdType.MESH
F32 = jnp.float32
BF16 = jnp.bfloat16
LANES = 128
ROWS = 64
CHIPS_Z = 8
LIMIT_MIB = 44


def dot(a, b, contract):
    return lax.dot_general(a, b, ((contract[:1], contract[1:]), ((), ())), preferred_element_type=F32)


def fused(
    seqs, zs, chs, grid,
    x_hbm, ct_hbm, right_hbm, left_hbm, gate1_hbm, gate2_hbm,
    ov, giv, gr_out, gl_out, gf_out, gs_out,
    xv, ctv, right, left, gate1, gate2,
    right_t, left_t, gate1_p, s1, flat, flat_out, prod, pair, grad_pair, section, gl, gr, gfirst, gsecond,
    fsend, frecv, bsend, brecv,
    csend, crecv, cgsend, cgrecv, half, xysend, xyrecv, ygsend, ygrecv, thin, zsend, zrecv, zgsend, zgrecv,
    in_sem, fs_sem, fr_sem, bs_sem, br_sem, r_sem,
):
    s, ch = lax.axis_index("seq"), lax.axis_index("ch")
    core = s % 2
    own, own_y, own_z = s // 2, s // (2 * zs), (s // 2) % zs
    ys = seqs // (2 * zs)
    pairs = seqs // 2
    blocks = grid // ROWS

    barrier = pltpu.get_barrier_semaphore()

    def turns(extent):
        return [(n + 1) // 2 if n % 2 else extent - n // 2 for n in reversed(range(1, extent))] + [0]

    def sweep(act, cores):
        far_z, far_y = turns(zs), turns(ys)
        for other in cores:
            c = 1 - core if other else core

            def row(y, offsets):
                base = y * (2 * zs) + c
                for dz in offsets:
                    act(base + 2 * lax.rem(own_z + dz, zs))

            for dy in far_y[:-1]:
                row(lax.rem(own_y + dy, ys), far_z)
            row(own_y, far_z if other else far_z[:-1])

    def greet(d):
        pl.semaphore_signal(barrier, inc=1, device_id=(d, ch), device_id_type=MESH)

    def greet_ch(t, _):
        x, y = (ch + 1 + t // ys) % chs, t % ys
        pl.semaphore_signal(barrier, inc=1, device_id=((y * zs + own_z) * 2 + core, x), device_id_type=MESH)
        return 0

    loads = [
        pltpu.make_async_copy(src, dst, in_sem.at[n])
        for n, (src, dst) in enumerate(
            ((x_hbm, xv), (right_hbm, right), (gate1_hbm, gate1), (ct_hbm, ctv), (left_hbm, left), (gate2_hbm, gate2))
        )
    ]
    for load in loads:
        load.start()
    sweep(greet, (True, False))
    lax.fori_loop(0, (chs - 1) * ys, greet_ch, 0)
    for load in loads[:3]:
        load.wait()

    def half_of(h):
        return slice(h * LANES, (h + 1) * LANES)

    def x_pair(h, ip):
        return jnp.concatenate([xv[2 * ip, :, half_of(h)], xv[2 * ip + 1, :, half_of(h)]], axis=1)

    def spread(h):
        pltpu.make_async_copy(fsend.at[h, s], frecv.at[h, s], fr_sem.at[h]).start()

        def send(d):
            pltpu.make_async_remote_copy(
                src_ref=fsend.at[h, d], dst_ref=frecv.at[h, s], send_sem=fs_sem.at[h], recv_sem=fr_sem.at[h],
                device_id=(d, ch), device_id_type=MESH,
            ).start()

        sweep(send, (True, False))

    def send_back(h):
        pltpu.make_async_copy(bsend.at[h, s], brecv.at[h, core, own], br_sem.at[h, 1]).start()
        for rel in range(2):

            def send(d):
                pltpu.make_async_remote_copy(
                    src_ref=bsend.at[h, d], dst_ref=brecv.at[h, core, own],
                    send_sem=bs_sem.at[h], recv_sem=br_sem.at[h, rel],
                    device_id=(d, ch), device_id_type=MESH,
                ).start()

            sweep(send, (rel == 0,))

    def arrived(dst, sem):
        pltpu.make_async_copy(dst, dst, sem).wait()

    def first_stage(h):
        def per_pair(ip, _):
            prod[...] = dot(right[...], x_pair(h, ip), (1, 0))

            def rows(b, _):
                r = pl.ds(pl.multiple_of(b * ROWS, ROWS), ROWS)
                gate = gate1[r, half_of(h)].astype(F32)
                for e in range(2):
                    rounded = prod[r, half_of(e)].astype(BF16).astype(F32)
                    flat[pl.ds(b * (ROWS * 8) + 2 * ip + e, ROWS, stride=8), :] = rounded * gate
                    rounded = rounded.reshape(ROWS // 16, 2, 8, LANES)
                    to = pl.ds(pl.multiple_of(b * (ROWS // 2), ROWS // 2), ROWS // 2)
                    for p in range(2):
                        s1[2 * ip + e, h, p, to, :] = rounded[:, p].reshape(ROWS // 2, LANES).astype(BF16)
                return 0

            lax.fori_loop(0, blocks, rows, 0)
            return 0

        lax.fori_loop(0, 4, per_pair, 0)

        def pack(d, _):
            rows = flat[pl.ds(pl.multiple_of(d * 64, 64), 64), :]
            fsend[h, d] = rows.reshape(8, 8, LANES).astype(BF16)
            return 0

        lax.fori_loop(0, seqs, pack, 0, unroll=4)

    def middle(h):
        def unpack(b, _):
            m = pl.ds(pl.multiple_of(b * 8, 8), 8)
            flat[pl.ds(pl.multiple_of(b * 64, 64), 64), :] = ctv[m, :, half_of(h)].astype(F32).reshape(64, LANES)
            return 0

        lax.fori_loop(0, grid // 8, unpack, 0, unroll=4)
        gsecond[:, half_of(h)] = jnp.zeros((grid, LANES), F32)
        arrived(frecv.at[h], fr_sem.at[h])

        def per_pair(kp, _):
            pair[...] = jnp.concatenate(
                [frecv[h, :, 2 * kp + e].astype(F32).reshape(grid, LANES).astype(BF16) for e in range(2)], axis=1
            )
            prod[...] = dot(left[...], pair[...], (1, 0))

            def rows(b, _):
                r = pl.ds(pl.multiple_of(b * ROWS, ROWS), ROWS)
                gate = gate2[r, half_of(h)].astype(F32)
                total = gsecond[r, half_of(h)]
                for e in range(2):
                    at = pl.ds(b * (ROWS * 8) + 2 * kp + e, ROWS, stride=8)
                    mixed = prod[r, half_of(e)]
                    grad_out = flat[at, :]
                    logistic = 1.0 / (1.0 + jnp.exp(-mixed))
                    activated = mixed * logistic
                    flat_out[at, :] = activated * gate
                    total = total + grad_out * activated
                    grad_mixed = grad_out * gate * logistic * (1.0 + mixed * (1.0 - logistic))
                    grad_pair[r, half_of(e)] = grad_mixed.astype(BF16)
                gsecond[r, half_of(h)] = total
                return 0

            lax.fori_loop(0, blocks, rows, 0)
            gl[...] += dot(grad_pair[...], pair[...], (1, 1))
            prod[...] = dot(left_t[...], grad_pair[...], (1, 0))
            for e in range(2):
                bsend[h, :, 2 * kp + e] = prod[:, half_of(e)].reshape(seqs, 8, LANES).astype(BF16)
            return 0

        lax.fori_loop(0, 4, per_pair, 0)

    def write_out(h):
        def pack(b, _):
            m = pl.ds(pl.multiple_of(b * 8, 8), 8)
            rows = flat_out[pl.ds(pl.multiple_of(b * 64, 64), 64), :]
            ov[m, :, half_of(h)] = rows.reshape(8, 8, LANES).astype(BF16)
            return 0

        lax.fori_loop(0, grid // 8, pack, 0, unroll=4)

    def parity(rel):
        return core if rel else 1 - core

    def last_stage(h, rel):
        p = parity(rel)
        arrived(brecv.at[h, p], br_sem.at[h, rel])

        def unpack(b, _):
            rows = brecv[h, p, b].astype(F32).reshape(64, LANES)
            flat[pl.ds(pl.multiple_of(b * 64, 64), 64), :] = rows
            return 0

        lax.fori_loop(0, pairs, unpack, 0, unroll=8)

        def per_pair(ip, _):
            def rows(b, _):
                r = pl.ds(pl.multiple_of(b * ROWS, ROWS), ROWS)
                gate = gate1_p[p, r, half_of(h)]
                total = gfirst[p, r, half_of(h)]
                for e in range(2):
                    grad = flat[pl.ds(b * (ROWS * 8) + 2 * ip + e, ROWS, stride=8), :]
                    total = total + grad * s1[2 * ip + e, h, p, r, :].astype(F32)
                    section[p, ip, r, half_of(e)] = (grad * gate).astype(BF16)
                gfirst[p, r, half_of(h)] = total
                return 0

            lax.fori_loop(0, blocks // 2, rows, 0, unroll=True)
            gr[p] += dot(section[p, ip], x_pair(h, ip), (1, 1))
            return 0

        lax.fori_loop(0, 4, per_pair, 0, unroll=True)

    def grad_of_inputs(h):
        def per_pair(ip, _):
            prod[...] = dot(right_t[0], section[0, ip], (1, 0)) + dot(right_t[1], section[1, ip], (1, 0))
            for e in range(2):
                giv[2 * ip + e, :, half_of(h)] = prod[:, half_of(e)].astype(BF16)
            return 0

        lax.fori_loop(0, 4, per_pair, 0, unroll=True)

    def to_peers(count, me, src, dst, send_sem, recv_sem, device):
        pltpu.make_async_copy(src.at[me], dst.at[me], recv_sem).start()
        for t in range(1, count):
            d = (me + t) % count
            pltpu.make_async_remote_copy(
                src_ref=src.at[d], dst_ref=dst.at[me], send_sem=send_sem, recv_sem=recv_sem,
                device_id=device(d), device_id_type=MESH,
            ).start()

    def at_xy(d):
        return ((d % ys * zs + own_z) * 2 + core, d // ys)

    def at_y(d):
        return ((d * zs + own_z) * 2 + core, ch)

    def at_z(d):
        return ((own_y * zs + d) * 2 + core, ch)

    def core_copies(n):
        return [
            pltpu.make_async_remote_copy(
                src_ref=src.at[n], dst_ref=dst.at[n], send_sem=r_sem.at[n, 2 * q], recv_sem=r_sem.at[n, 2 * q + 1],
                device_id=(s + 1 - 2 * core, ch), device_id_type=MESH,
            )
            for q, (src, dst) in enumerate(((csend, crecv), (cgsend, cgrecv)))
        ]

    def reduce_core(n, rows):
        def give(q, _):
            csend[n, q], cgsend[n, q] = (part.astype(BF16) for part in rows(1 - core, q))
            return 0

        lax.fori_loop(0, pairs, give, 0, unroll=4)
        for copy in core_copies(n):
            copy.start()

    def reduce_xy(n, rows):
        for copy in core_copies(n):
            copy.wait()

        def take(q, _):
            matrix, gates = rows(core, q)
            total = matrix + crecv[n, q].astype(F32)
            for c in range(4):
                half[c, pl.ds(pl.multiple_of(q * 8, 8), 8), :] = total[:, c * LANES : (c + 1) * LANES]
            ygsend[n, q // zs, q % zs] = (gates + cgrecv[n, q].astype(F32)).astype(BF16)
            return 0

        lax.fori_loop(0, pairs, take, 0, unroll=8)
        for a in range(chs):
            for b in range(2):
                for c in range(4):
                    lanes = slice(c * LANES, (c + 1) * LANES)
                    part = half[c, pl.ds(2 * a + b, pairs, stride=8), :]
                    for y in range(ys):
                        xysend[n, a * ys + y, b, :, lanes] = part[y * zs : (y + 1) * zs].astype(BF16)
        to_peers(chs * ys, ch * ys + own_y, xysend.at[n], xyrecv.at[n], r_sem.at[n, 4], r_sem.at[n, 5], at_xy)
        to_peers(ys, own_y, ygsend.at[n], ygrecv.at[n], r_sem.at[n, 6], r_sem.at[n, 7], at_y)

    def reduce_z_gates(n):
        arrived(ygrecv.at[n], r_sem.at[n, 7])
        total = ygrecv[n, 0].astype(F32)
        for a in range(1, ys):
            total = total + ygrecv[n, a].astype(F32)
        zgsend[n] = total.astype(BF16)
        to_peers(zs, own_z, zgsend.at[n], zgrecv.at[n], r_sem.at[n, 8], r_sem.at[n, 9], at_z)

    def reduce_z(n):
        arrived(xyrecv.at[n], r_sem.at[n, 5])
        total = xyrecv[n, 0].astype(F32)
        for a in range(1, chs * ys):
            total = total + xyrecv[n, a].astype(F32)
        total = total.reshape(2 * zs, grid)
        for c in range(4):
            thin[c] = total[:, c * LANES : (c + 1) * LANES]
        for p in range(zs):
            for c in range(4):
                zsend[n, p, :, c * LANES : (c + 1) * LANES] = thin[c, pl.ds(p, 2, stride=zs), :].astype(BF16)
        to_peers(zs, own_z, zsend.at[n], zrecv.at[n], r_sem.at[n, 10], r_sem.at[n, 11], at_z)

    def finish(n, matrix_out, gates_out):
        arrived(zgrecv.at[n], r_sem.at[n, 9])
        gates_out[...] = jnp.sum(zgrecv[n].astype(F32), axis=0)
        arrived(zrecv.at[n], r_sem.at[n, 11])
        matrix_out[...] = jnp.sum(zrecv[n].astype(F32), axis=0)
        for buffer, count, sem in (
            (xysend, chs * ys, 4), (ygsend, ys, 6), (zgsend, zs, 8), (zsend, zs, 10)
        ):
            arrived(buffer.at[n, pl.ds(0, count - 1)], r_sem.at[n, sem])

    def left_rows(p, q):
        r = pl.ds(pl.multiple_of(q * 16 + p * 8, 8), 8)
        return gl[r, :], gsecond[r, :]

    def right_rows_of(p, q):
        r = pl.ds(pl.multiple_of(q * 8, 8), 8)
        return gr[p, r, :], gfirst[p, r, :]

    first_stage(0)
    pl.semaphore_wait(barrier, seqs - 1 + (chs - 1) * ys)
    spread(0)
    first_stage(1)
    spread(1)
    for load in loads[3:]:
        load.wait()
    right_rows = right[...].astype(F32).reshape(pairs, 2, 8, grid)
    for p in range(2):
        right_t[p] = right_rows[:, p].reshape(grid // 2, grid).astype(BF16).T

    def split_gate(q, _):
        rows = gate1[pl.ds(pl.multiple_of(q * 16, 16), 16), :].astype(F32)
        for p in range(2):
            gate1_p[p, pl.ds(pl.multiple_of(q * 8, 8), 8), :] = rows[p * 8 : p * 8 + 8]
        return 0

    lax.fori_loop(0, pairs, split_gate, 0)
    gfirst[...] = jnp.zeros(gfirst.shape, F32)
    left_t[...] = left[...].T
    gl[...] = jnp.zeros(gl.shape, F32)
    gr[...] = jnp.zeros(gr.shape, F32)
    for h in range(2):
        middle(h)
        send_back(h)
        if h == 1:
            reduce_core(0, left_rows)
        write_out(h)
    reduce_xy(0, left_rows)
    last_stage(0, 0)
    last_stage(0, 1)
    grad_of_inputs(0)
    last_stage(1, 0)
    reduce_core(1, right_rows_of)
    reduce_z_gates(0)
    reduce_z(0)
    last_stage(1, 1)
    reduce_xy(1, right_rows_of)
    grad_of_inputs(1)
    reduce_z_gates(1)
    reduce_z(1)
    finish(0, gl_out, gs_out)
    finish(1, gr_out, gf_out)
    for h in range(2):
        arrived(fsend.at[h, pl.ds(0, seqs - 1)], fs_sem.at[h])
        arrived(bsend.at[h, pl.ds(0, seqs - 1)], bs_sem.at[h])


def place(*refs):
    count = len(refs) // 2
    sems = refs[-1]
    copies = []
    for q in range(count):
        cuts = 4 if q < 2 else 1
        rows = refs[q].shape[0] // cuts
        for n in range(cuts):
            at = pl.ds(n * rows, rows)
            copies.append(
                pltpu.make_async_copy(refs[q].at[at], refs[count + q].at[at], sems.at[len(copies)])
            )
    for copy in copies:
        copy.start()
    for copy in copies:
        copy.wait()


def per_device(seqs, zs, chs, inputs, cotangent, right_weight, left_weight, first_gate, second_gate):
    rows, grid, width = inputs.shape
    any_space = pl.BlockSpec(memory_space=pl.ANY)
    hbm = pl.BlockSpec(memory_space=pltpu.HBM)
    vmem = pl.BlockSpec(memory_space=pltpu.VMEM)
    pairs, ys = seqs // 2, seqs // (2 * zs)
    block = (2, seqs, 8, 8, LANES)

    def v(shape, dtype=BF16):
        return pltpu.VMEM(shape, dtype)

    def twice(*shape):
        return [pltpu.VMEM((2,) + shape, BF16)] * 2

    dma = pltpu.SemaphoreType.DMA
    shapes = (
        jax.ShapeDtypeStruct(cotangent.shape, BF16),
        jax.ShapeDtypeStruct(inputs.shape, BF16),
        jax.ShapeDtypeStruct((2, grid), F32),
        jax.ShapeDtypeStruct((2, grid), F32),
        jax.ShapeDtypeStruct((8, width), F32),
        jax.ShapeDtypeStruct((8, width), F32),
    )
    results = pl.pallas_call(
        functools.partial(fused, seqs, zs, chs, grid),
        out_shape=shapes,
        in_specs=[hbm] * 6,
        out_specs=(vmem,) * 6,
        scratch_shapes=[
            v(inputs.shape), v(cotangent.shape), v((grid, grid)), v((grid, grid)), v((grid, width)), v((grid, width)),
            v((2, grid, grid // 2)), v((grid, grid)), v((2, grid // 2, width), F32), v((8, 2, 2, grid // 2, LANES)), v((grid * 8, LANES), F32), v((grid * 8, LANES), F32),
            v((grid, 2 * LANES), F32), v((grid, 2 * LANES)), v((grid, 2 * LANES)), v((2, 4, grid // 2, 2 * LANES)),
            v((grid, grid), F32), v((2, grid // 2, grid), F32), v((2, grid // 2, width), F32), v((grid, width), F32),
            v(block), v(block), v(block), v((2, 2, pairs, 8, 8, LANES)),
            *twice(pairs, 8, grid), *twice(pairs, 8, width),
            v((4, pairs * 8, LANES), F32), *twice(chs * ys, 2, zs, grid),
            *twice(ys, zs, 8, width),
            v((4, 2 * zs, LANES), F32), *twice(zs, 2, grid), *twice(zs, 8, width),
            dma((6,)), dma((2,)), dma((2,)), dma((2,)), dma((2, 2)), dma((2, 12)),
        ],
        compiler_params=pltpu.CompilerParams(
            collective_id=0, has_side_effects=True, vmem_limit_bytes=LIMIT_MIB * 1024 * 1024
        ),
    )(*(
        pltpu.with_memory_space_constraint(array, pltpu.HBM)
        for array in (inputs, cotangent, right_weight, left_weight, first_gate, second_gate)
    ))
    return pl.pallas_call(
        place,
        out_shape=shapes,
        in_specs=[any_space] * 6,
        out_specs=(hbm,) * 6,
        scratch_shapes=[dma((12,))],
        compiler_params=pltpu.CompilerParams(vmem_limit_bytes=4 * 1024 * 1024),
    )(*results)


def solution(mesh):
    placed = (P("seq", None, "ch"), P(None, "seq", "ch"), P(), P(), P(None, "ch"), P(None, "ch"))
    return jax.shard_map(
        functools.partial(per_device, mesh.shape["seq"], CHIPS_Z, mesh.shape["ch"]),
        mesh=mesh,
        in_specs=placed,
        out_specs=(
            P(None, "seq", "ch"),
            P("seq", None, "ch"),
            P(("seq", "ch"), None),
            P(("seq", "ch"), None),
            P("seq", "ch"),
            P("seq", "ch"),
        ),
        check_vma=False,
    )
```

```python
import functools

import jax
import jax.numpy as jnp
from jax import lax
from jax.experimental import pallas as pl
from jax.experimental.pallas import tpu as pltpu
from jax.sharding import PartitionSpec as P

MESH = pl.DeviceIdType.MESH
F32 = jnp.float32
BF16 = jnp.bfloat16
LANES = 128
ROWS = 64
CHIPS_Z = 8
LIMIT_MIB = 44


def dot(a, b, contract):
    return lax.dot_general(a, b, ((contract[:1], contract[1:]), ((), ())), preferred_element_type=F32)


def fused(
    seqs, zs, chs, grid,
    x_hbm, ct_hbm, right_hbm, left_hbm, gate1_hbm, gate2_hbm,
    ov, giv, gr_out, gl_out, gf_out, gs_out,
    xv, ctv, right, left, gate1, gate2,
    right_t, left_t, gate1_p, s1, flat, flat_out, prod, pair, grad_pair, section, gl, gr, gfirst, gsecond,
    fsend, frecv, bsend, brecv,
    csend, crecv, cgsend, cgrecv, half, xysend, xyrecv, ygsend, ygrecv, thin, zsend, zrecv, zgsend, zgrecv,
    in_sem, fs_sem, fr_sem, bs_sem, br_sem, r_sem,
):
    s, ch = lax.axis_index("seq"), lax.axis_index("ch")
    core = s % 2
    own, own_y, own_z = s // 2, s // (2 * zs), (s // 2) % zs
    ys = seqs // (2 * zs)
    pairs = seqs // 2
    blocks = grid // ROWS
    quads, part_rows = seqs // 4, grid // 4
    z_class = own_z % 2

    barrier = pltpu.get_barrier_semaphore()

    def turns(extent):
        return [(n + 1) // 2 if n % 2 else extent - n // 2 for n in reversed(range(1, extent))] + [0]

    def sweep(act, other, offsets):
        far_y = turns(ys)
        c = 1 - core if other else core

        def row(y, distances):
            base = y * (2 * zs) + c
            for dz in distances:
                act(base + 2 * lax.rem(own_z + dz, zs))

        for dy in far_y[:-1]:
            row(lax.rem(own_y + dy, ys), offsets)
        row(own_y, offsets if other else [dz for dz in offsets if dz])

    far_z = turns(zs)
    odd_z, even_z = [dz for dz in far_z if dz % 2], [dz for dz in far_z if dz % 2 == 0]

    def greet(d):
        pl.semaphore_signal(barrier, inc=1, device_id=(d, ch), device_id_type=MESH)

    def greet_ch(t, _):
        x, y = (ch + 1 + t // ys) % chs, t % ys
        pl.semaphore_signal(barrier, inc=1, device_id=((y * zs + own_z) * 2 + core, x), device_id_type=MESH)
        return 0

    loads = [
        pltpu.make_async_copy(src, dst, in_sem.at[n])
        for n, (src, dst) in enumerate(
            ((x_hbm, xv), (right_hbm, right), (gate1_hbm, gate1), (ct_hbm, ctv), (left_hbm, left), (gate2_hbm, gate2))
        )
    ]
    for load in loads:
        load.start()
    for other in (True, False):
        sweep(greet, other, far_z)
    lax.fori_loop(0, (chs - 1) * ys, greet_ch, 0)
    for load in loads[:3]:
        load.wait()

    def half_of(h):
        return slice(h * LANES, (h + 1) * LANES)

    def x_pair(h, ip):
        return jnp.concatenate([xv[2 * ip, :, half_of(h)], xv[2 * ip + 1, :, half_of(h)]], axis=1)

    def spread(h):
        pltpu.make_async_copy(fsend.at[h, s], frecv.at[h, s], fr_sem.at[h]).start()

        def send(d):
            pltpu.make_async_remote_copy(
                src_ref=fsend.at[h, d], dst_ref=frecv.at[h, s], send_sem=fs_sem.at[h], recv_sem=fr_sem.at[h],
                device_id=(d, ch), device_id_type=MESH,
            ).start()

        for other in (True, False):
            sweep(send, other, far_z)

    def send_back(h, parts):
        mine = z_class * quads + s // 4
        if 2 in parts:
            pltpu.make_async_copy(bsend.at[h, s], brecv.at[h, core, mine], br_sem.at[h, 2]).start()
        for part in parts:
            other, offsets = ((True, far_z), (False, odd_z), (False, even_z))[part]

            def send(d):
                pltpu.make_async_remote_copy(
                    src_ref=bsend.at[h, d], dst_ref=brecv.at[h, core, mine],
                    send_sem=bs_sem.at[h], recv_sem=br_sem.at[h, part],
                    device_id=(d, ch), device_id_type=MESH,
                ).start()

            sweep(send, other, offsets)

    def arrived(dst, sem):
        pltpu.make_async_copy(dst, dst, sem).wait()

    def first_stage(h):
        def per_pair(ip, _):
            prod[...] = dot(right[...], x_pair(h, ip), (1, 0))

            def rows(b, _):
                r = pl.ds(pl.multiple_of(b * ROWS, ROWS), ROWS)
                gate = gate1[r, half_of(h)].astype(F32)
                for e in range(2):
                    rounded = prod[r, half_of(e)].astype(BF16).astype(F32)
                    flat[pl.ds(b * (ROWS * 8) + 2 * ip + e, ROWS, stride=8), :] = rounded * gate
                    rounded = rounded.reshape(ROWS // 32, 2, 2, 8, LANES)
                    for zp in range(2):
                        to = pl.ds(pl.multiple_of(zp * part_rows + b * (ROWS // 4), ROWS // 4), ROWS // 4)
                        for p in range(2):
                            s1[2 * ip + e, h, p, to, :] = rounded[:, zp, p].reshape(ROWS // 4, LANES).astype(BF16)
                return 0

            lax.fori_loop(0, blocks, rows, 0)
            return 0

        lax.fori_loop(0, 4, per_pair, 0)

        def pack(d, _):
            rows = flat[pl.ds(pl.multiple_of(d * 64, 64), 64), :]
            fsend[h, d] = rows.reshape(8, 8, LANES).astype(BF16)
            return 0

        lax.fori_loop(0, seqs, pack, 0, unroll=4)

    def middle(h):
        def unpack(b, _):
            m = pl.ds(pl.multiple_of(b * 8, 8), 8)
            flat[pl.ds(pl.multiple_of(b * 64, 64), 64), :] = ctv[m, :, half_of(h)].astype(F32).reshape(64, LANES)
            return 0

        lax.fori_loop(0, grid // 8, unpack, 0, unroll=4)
        gsecond[:, half_of(h)] = jnp.zeros((grid, LANES), F32)
        arrived(frecv.at[h], fr_sem.at[h])

        def per_pair(kp, _):
            pair[...] = jnp.concatenate(
                [frecv[h, :, 2 * kp + e].astype(F32).reshape(grid, LANES).astype(BF16) for e in range(2)], axis=1
            )
            prod[...] = dot(left[...], pair[...], (1, 0))

            def rows(b, _):
                r = pl.ds(pl.multiple_of(b * ROWS, ROWS), ROWS)
                gate = gate2[r, half_of(h)].astype(F32)
                total = gsecond[r, half_of(h)]
                for e in range(2):
                    at = pl.ds(b * (ROWS * 8) + 2 * kp + e, ROWS, stride=8)
                    mixed = prod[r, half_of(e)]
                    grad_out = flat[at, :]
                    logistic = 1.0 / (1.0 + jnp.exp(-mixed))
                    activated = mixed * logistic
                    flat_out[at, :] = activated * gate
                    total = total + grad_out * activated
                    grad_mixed = grad_out * gate * logistic * (1.0 + mixed * (1.0 - logistic))
                    grad_pair[r, half_of(e)] = grad_mixed.astype(BF16)
                gsecond[r, half_of(h)] = total
                return 0

            lax.fori_loop(0, blocks, rows, 0)
            gl[...] += dot(grad_pair[...], pair[...], (1, 1))
            prod[...] = dot(left_t[...], grad_pair[...], (1, 0))
            for e in range(2):
                bsend[h, :, 2 * kp + e] = prod[:, half_of(e)].reshape(seqs, 8, LANES).astype(BF16)
            return 0

        lax.fori_loop(0, 4, per_pair, 0)

    def write_out(h):
        def pack(b, _):
            m = pl.ds(pl.multiple_of(b * 8, 8), 8)
            rows = flat_out[pl.ds(pl.multiple_of(b * 64, 64), 64), :]
            ov[m, :, half_of(h)] = rows.reshape(8, 8, LANES).astype(BF16)
            return 0

        lax.fori_loop(0, grid // 8, pack, 0, unroll=4)

    def class_of(order):
        return z_class if order else 1 - z_class

    def rows_arrived(h, part):
        if part == 0:
            arrived(brecv.at[h, 1 - core], br_sem.at[h, 0])
        else:
            at = pl.ds(class_of(part - 1) * quads, quads)
            arrived(brecv.at[h, core, at], br_sem.at[h, part])

    def last_stage(h, p, first, count):
        def unpack(b, _):
            rows = brecv[h, p, first * quads + b].astype(F32).reshape(64, LANES)
            flat[pl.ds(pl.multiple_of(b * 64, 64), 64), :] = rows
            return 0

        lax.fori_loop(0, count * quads, unpack, 0, unroll=8)
        whole = pl.ds(pl.multiple_of(first * part_rows, part_rows), count * part_rows)

        def per_pair(ip, _):
            def rows(b, _):
                r = pl.ds(pl.multiple_of(first * part_rows + b * ROWS, ROWS), ROWS)
                gate = gate1_p[p, r, half_of(h)]
                total = gfirst[p, r, half_of(h)]
                for e in range(2):
                    grad = flat[pl.ds(b * (ROWS * 8) + 2 * ip + e, ROWS, stride=8), :]
                    total = total + grad * s1[2 * ip + e, h, p, r, :].astype(F32)
                    section[p, ip, r, half_of(e)] = (grad * gate).astype(BF16)
                gfirst[p, r, half_of(h)] = total
                return 0

            lax.fori_loop(0, count * part_rows // ROWS, rows, 0, unroll=True)
            gr[p, whole, :] += dot(section[p, ip, whole, :], x_pair(h, ip), (1, 1))
            return 0

        lax.fori_loop(0, 4, per_pair, 0, unroll=True)

    def grad_of_inputs(h):
        def per_pair(ip, _):
            prod[...] = dot(right_t[0], section[0, ip], (1, 0)) + dot(right_t[1], section[1, ip], (1, 0))
            for e in range(2):
                giv[2 * ip + e, :, half_of(h)] = prod[:, half_of(e)].astype(BF16)
            return 0

        lax.fori_loop(0, 4, per_pair, 0, unroll=True)

    def to_peers(count, me, src, dst, send_sem, recv_sem, device):
        pltpu.make_async_copy(src.at[me], dst.at[me], recv_sem).start()
        for t in range(1, count):
            d = (me + t) % count
            pltpu.make_async_remote_copy(
                src_ref=src.at[d], dst_ref=dst.at[me], send_sem=send_sem, recv_sem=recv_sem,
                device_id=device(d), device_id_type=MESH,
            ).start()

    def at_xy(d):
        return ((d % ys * zs + own_z) * 2 + core, d // ys)

    def at_y(d):
        return ((d * zs + own_z) * 2 + core, ch)

    def at_z(d):
        return ((own_y * zs + d) * 2 + core, ch)

    def core_copies(n):
        return [
            pltpu.make_async_remote_copy(
                src_ref=src.at[n], dst_ref=dst.at[n], send_sem=r_sem.at[n, 2 * q], recv_sem=r_sem.at[n, 2 * q + 1],
                device_id=(s + 1 - 2 * core, ch), device_id_type=MESH,
            )
            for q, (src, dst) in enumerate(((csend, crecv), (cgsend, cgrecv)))
        ]

    def reduce_core(n, rows):
        def give(q, _):
            csend[n, q], cgsend[n, q] = (part.astype(BF16) for part in rows(1 - core, q))
            return 0

        lax.fori_loop(0, pairs, give, 0, unroll=4)
        for copy in core_copies(n):
            copy.start()

    def core_arrived(n):
        for copy in core_copies(n):
            copy.wait()

    def reduce_xy(n, rows, order):
        def take(q2, _):
            q = 2 * q2 + class_of(order)
            matrix, gates = rows(core, q)
            total = matrix + crecv[n, q].astype(F32)
            for c in range(4):
                half[c, pl.ds(pl.multiple_of(q2 * 8, 8), 8), :] = total[:, c * LANES : (c + 1) * LANES]
            ygsend[n, q // zs, q % zs] = (gates + cgrecv[n, q].astype(F32)).astype(BF16)
            return 0

        lax.fori_loop(0, quads, take, 0, unroll=8)
        for a in range(chs):
            for y in range(ys):
                for b in range(2):
                    for c in range(4):
                        part = half[c, pl.ds(y * (4 * zs) + 2 * a + b, zs // 2, stride=8), :]
                        xysend[n, order, a * ys + y, b, :, c * LANES : (c + 1) * LANES] = part.astype(BF16)
        to_peers(
            chs * ys, ch * ys + own_y, xysend.at[n, order], xyrecv.at[n, order],
            r_sem.at[n, 4 + 8 * order], r_sem.at[n, 5 + 8 * order], at_xy,
        )
        if order:
            to_peers(ys, own_y, ygsend.at[n], ygrecv.at[n], r_sem.at[n, 6], r_sem.at[n, 7], at_y)

    def reduce_z_gates(n):
        arrived(ygrecv.at[n], r_sem.at[n, 7])
        total = ygrecv[n, 0].astype(F32)
        for a in range(1, ys):
            total = total + ygrecv[n, a].astype(F32)
        zgsend[n] = total.astype(BF16)
        to_peers(zs, own_z, zgsend.at[n], zgrecv.at[n], r_sem.at[n, 8], r_sem.at[n, 9], at_z)

    def reduce_z(n, order):
        arrived(xyrecv.at[n, order], r_sem.at[n, 5 + 8 * order])
        total = xyrecv[n, order, 0].astype(F32)
        for a in range(1, chs * ys):
            total = total + xyrecv[n, order, a].astype(F32)
        for c in range(4):
            for b in range(2):
                thin[c, b * 8 : b * 8 + zs // 2, :] = total[b, :, c * LANES : (c + 1) * LANES]
        for p in range(zs // 2):
            for c in range(4):
                to = 2 * p + class_of(order)
                zsend[n, to, :, c * LANES : (c + 1) * LANES] = thin[c, pl.ds(p, 2, stride=8), :].astype(BF16)
        for t in range(zs // 2):
            d = (own_z + 2 * t + 1 - order) % zs
            if order and t == 0:
                pltpu.make_async_copy(zsend.at[n, own_z], zrecv.at[n, own_z], r_sem.at[n, 11]).start()
            else:
                pltpu.make_async_remote_copy(
                    src_ref=zsend.at[n, d], dst_ref=zrecv.at[n, own_z],
                    send_sem=r_sem.at[n, 10], recv_sem=r_sem.at[n, 11],
                    device_id=at_z(d), device_id_type=MESH,
                ).start()

    def finish(n, matrix_out, gates_out):
        arrived(zgrecv.at[n], r_sem.at[n, 9])
        gates_out[...] = jnp.sum(zgrecv[n].astype(F32), axis=0)
        arrived(zrecv.at[n], r_sem.at[n, 11])
        matrix_out[...] = jnp.sum(zrecv[n].astype(F32), axis=0)
        for order in range(2):
            arrived(xysend.at[n, order, pl.ds(0, chs * ys - 1)], r_sem.at[n, 4 + 8 * order])
        for buffer, count, sem in ((ygsend, ys, 6), (zgsend, zs, 8), (zsend, zs, 10)):
            arrived(buffer.at[n, pl.ds(0, count - 1)], r_sem.at[n, sem])

    def left_rows(p, q):
        r = pl.ds(pl.multiple_of(q * 16 + p * 8, 8), 8)
        return gl[r, :], gsecond[r, :]

    def right_rows_of(p, q):
        r = pl.ds(pl.multiple_of(q % 2 * part_rows + q // 2 * 8, 8), 8)
        return gr[p, r, :], gfirst[p, r, :]

    first_stage(0)
    pl.semaphore_wait(barrier, seqs - 1 + (chs - 1) * ys)
    spread(0)
    first_stage(1)
    spread(1)
    for load in loads[3:]:
        load.wait()
    right_rows = right[...].astype(F32).reshape(quads, 2, 2, 8, grid)
    for p in range(2):
        both = jnp.concatenate([right_rows[:, zp, p].reshape(part_rows, grid) for zp in range(2)], axis=0)
        right_t[p] = both.astype(BF16).T

    def split_gate(q, _):
        rows = gate1[pl.ds(pl.multiple_of(q * 32, 32), 32), :].astype(F32)
        for n in range(4):
            to = pl.ds(pl.multiple_of(n // 2 * part_rows + q * 8, 8), 8)
            gate1_p[n % 2, to, :] = rows[n * 8 : n * 8 + 8]
        return 0

    lax.fori_loop(0, quads, split_gate, 0)
    gfirst[...] = jnp.zeros(gfirst.shape, F32)
    left_t[...] = left[...].T
    gl[...] = jnp.zeros(gl.shape, F32)
    gr[...] = jnp.zeros(gr.shape, F32)
    for h in range(2):
        middle(h)
        send_back(h, (0,) if h else (0, 1, 2))
        if h == 1:
            reduce_core(0, left_rows)
        write_out(h)
    core_arrived(0)
    for order in range(2):
        reduce_xy(0, left_rows, order)
    rows_arrived(0, 0)
    last_stage(0, 1 - core, 0, 2)
    rows_arrived(0, 1)
    rows_arrived(0, 2)
    send_back(1, (1,))
    last_stage(0, core, 0, 2)
    grad_of_inputs(0)
    rows_arrived(1, 0)
    send_back(1, (2,))
    last_stage(1, 1 - core, 0, 2)
    reduce_core(1, right_rows_of)
    reduce_z_gates(0)
    for order in range(2):
        reduce_z(0, order)
    core_arrived(1)
    for order in range(2):
        rows_arrived(1, order + 1)
        last_stage(1, core, class_of(order), 1)
        reduce_xy(1, right_rows_of, order)
    reduce_z(1, 0)
    grad_of_inputs(1)
    finish(0, gl_out, gs_out)
    reduce_z_gates(1)
    reduce_z(1, 1)
    finish(1, gr_out, gf_out)
    for h in range(2):
        arrived(fsend.at[h, pl.ds(0, seqs - 1)], fs_sem.at[h])
        arrived(bsend.at[h, pl.ds(0, seqs - 1)], bs_sem.at[h])


def place(*refs):
    count = len(refs) // 2
    sems = refs[-1]
    copies = []
    for q in range(count):
        cuts = 4 if q < 2 else 1
        rows = refs[q].shape[0] // cuts
        for n in range(cuts):
            at = pl.ds(n * rows, rows)
            copies.append(
                pltpu.make_async_copy(refs[q].at[at], refs[count + q].at[at], sems.at[len(copies)])
            )
    for copy in copies:
        copy.start()
    for copy in copies:
        copy.wait()


def per_device(seqs, zs, chs, inputs, cotangent, right_weight, left_weight, first_gate, second_gate):
    rows, grid, width = inputs.shape
    any_space = pl.BlockSpec(memory_space=pl.ANY)
    hbm = pl.BlockSpec(memory_space=pltpu.HBM)
    vmem = pl.BlockSpec(memory_space=pltpu.VMEM)
    pairs, ys = seqs // 2, seqs // (2 * zs)
    block = (2, seqs, 8, 8, LANES)

    def v(shape, dtype=BF16):
        return pltpu.VMEM(shape, dtype)

    def twice(*shape):
        return [pltpu.VMEM((2,) + shape, BF16)] * 2

    dma = pltpu.SemaphoreType.DMA
    shapes = (
        jax.ShapeDtypeStruct(cotangent.shape, BF16),
        jax.ShapeDtypeStruct(inputs.shape, BF16),
        jax.ShapeDtypeStruct((2, grid), F32),
        jax.ShapeDtypeStruct((2, grid), F32),
        jax.ShapeDtypeStruct((8, width), F32),
        jax.ShapeDtypeStruct((8, width), F32),
    )
    results = pl.pallas_call(
        functools.partial(fused, seqs, zs, chs, grid),
        out_shape=shapes,
        in_specs=[hbm] * 6,
        out_specs=(vmem,) * 6,
        scratch_shapes=[
            v(inputs.shape), v(cotangent.shape), v((grid, grid)), v((grid, grid)), v((grid, width)), v((grid, width)),
            v((2, grid, grid // 2)), v((grid, grid)), v((2, grid // 2, width), F32), v((8, 2, 2, grid // 2, LANES)), v((grid * 8, LANES), F32), v((grid * 8, LANES), F32),
            v((grid, 2 * LANES), F32), v((grid, 2 * LANES)), v((grid, 2 * LANES)), v((2, 4, grid // 2, 2 * LANES)),
            v((grid, grid), F32), v((2, grid // 2, grid), F32), v((2, grid // 2, width), F32), v((grid, width), F32),
            v(block), v(block), v(block), v((2, 2, pairs, 8, 8, LANES)),
            *twice(pairs, 8, grid), *twice(pairs, 8, width),
            v((4, pairs * 8, LANES), F32), *twice(2, chs * ys, 2, zs // 2, grid),
            *twice(ys, zs, 8, width),
            v((4, 2 * zs, LANES), F32), *twice(zs, 2, grid), *twice(zs, 8, width),
            dma((6,)), dma((2,)), dma((2,)), dma((2,)), dma((2, 3)), dma((2, 14)),
        ],
        compiler_params=pltpu.CompilerParams(
            collective_id=0, has_side_effects=True, vmem_limit_bytes=LIMIT_MIB * 1024 * 1024
        ),
    )(*(
        pltpu.with_memory_space_constraint(array, pltpu.HBM)
        for array in (inputs, cotangent, right_weight, left_weight, first_gate, second_gate)
    ))
    return pl.pallas_call(
        place,
        out_shape=shapes,
        in_specs=[any_space] * 6,
        out_specs=(hbm,) * 6,
        scratch_shapes=[dma((12,))],
        compiler_params=pltpu.CompilerParams(vmem_limit_bytes=4 * 1024 * 1024),
    )(*results)


def solution(mesh):
    placed = (P("seq", None, "ch"), P(None, "seq", "ch"), P(), P(), P(None, "ch"), P(None, "ch"))
    return jax.shard_map(
        functools.partial(per_device, mesh.shape["seq"], CHIPS_Z, mesh.shape["ch"]),
        mesh=mesh,
        in_specs=placed,
        out_specs=(
            P(None, "seq", "ch"),
            P("seq", None, "ch"),
            P(("seq", "ch"), None),
            P(("seq", "ch"), None),
            P("seq", "ch"),
            P("seq", "ch"),
        ),
        check_vma=False,
    )
```
